256 devices in a mesh: gy: 32 (over z, y), gz: 8 (over x, core).
Axes of the slice: x: 4, y: 4, z: 8, core: 2. Of those that a mesh axis runs over, the one named last changes fastest.
Arguments:
- wavefunction: float32 [2, 8, 4096, 2048], P(None, None, 'gy', 'gz'), may hold values from -6 to 6
- absorber: float32 [8, 4096, 2048], P(None, 'gy', 'gz'), may hold values from 0.05 to 1.5
- row_inverse: float32 [2, 4096, 128], P(None, 'gy'), may hold values from -1 to 1
- column_inverse: float32 [2, 2048, 256], replicated, may hold values from -1 to 1
- link_terms: float32 [2, 2, 2], replicated, may hold values from 0.65 to 0.7
- shell_blocks: int32 [8, 32, 56], P('gz'), may hold values from 0 to 63, as said below
- owner_map: int32 [8, 32, 56, 1], P('gz'), may hold values from 0 to 31; in each aligned block of 56 rows (0 to 55, 56 to 111, ..., all dimensions but the last counted through in order) at most 4 rows name the same one
- volkov_phase: float32 [128, 128], replicated, may hold values from -3.140625 to 3.140625
Outputs:
- damped: float32 [2, 8, 4096, 2048], P(None, None, 'gy', 'gz')
- spectrum: float32 [2, 256, 1024, 128], P(None, 'gy', 'gz')
The draws below stay inside these ranges and needn't reach their ends.
Inputs may be any that keep to these rules, and one draw needn't show every extreme that they name: `shell_blocks`: the ids listed for one device are distinct. `owner_map`: at most 4 of one device's listed blocks name the same owner.
All inputs are finite; a program needn't handle non-finite values.
Results may differ from the reference program's by a relative error of at most 0.0003.
Values sent between devices are 32-bit elements; how exact they have to be, the bound alone decides.
A program may use at most 64 MiB of HBM per device.

```python
import math
import jax
import jax.numpy as jnp
import numpy as np
from jax import lax

NX = 8
CY = 128
CZ = 256
BY = 2
KY = 128
KZ = 128
BPD = 64
SHELL_DEV = 56
CAP = 4
NY = 4096
NZ = 2048
N_GY = 32
N_GZ = 8


def draw_inverse(base_key, groups, length):
    subkeys = jax.random.split(base_key, 7)
    modulus = jax.random.uniform(subkeys[0], (groups, length), jnp.float32, 0.4, 0.8)
    phases = jax.random.uniform(subkeys[1], (groups, length), jnp.float32, -jnp.pi, jnp.pi)
    corner_phase = jax.random.uniform(subkeys[3], (groups, 2), jnp.float32, -jnp.pi, jnp.pi)
    edge_modulus = jax.random.uniform(subkeys[4], (groups, 2), jnp.float32, 0.004, 0.01)
    edge_phase = jax.random.uniform(subkeys[6], (groups, 2), jnp.float32, -jnp.pi, jnp.pi)
    spread = jax.random.uniform(subkeys[2], (2, groups, length, length), jnp.float32, -0.1, 0.1)
    corner_modulus = jax.random.uniform(subkeys[5], (groups, 2), jnp.float32, 0.95, 0.99)
    identity = jnp.eye(length, dtype=jnp.float32)
    off_diagonal = spread * (1.0 - identity)
    real_part = off_diagonal[0] + (modulus * jnp.cos(phases))[:, :, None] * identity
    imag_part = off_diagonal[1] + (modulus * jnp.sin(phases))[:, :, None] * identity
    places = jnp.arange(length, dtype=jnp.int32)
    first = places == 0
    last = places == length - 1
    lower_corner = (last[:, None] & first[None, :])[None]
    upper_corner = (first[:, None] & last[None, :])[None]
    head_diagonal = (first[:, None] & first[None, :])[None]
    tail_diagonal = (last[:, None] & last[None, :])[None]
    corner_real = corner_modulus * jnp.cos(corner_phase)
    corner_imag = corner_modulus * jnp.sin(corner_phase)
    edge_real = edge_modulus * jnp.cos(edge_phase)
    edge_imag = edge_modulus * jnp.sin(edge_phase)
    real_part = jnp.where(lower_corner, corner_real[:, 0, None, None], real_part)
    real_part = jnp.where(upper_corner, corner_real[:, 1, None, None], real_part)
    real_part = jnp.where(head_diagonal, edge_real[:, 0, None, None], real_part)
    real_part = jnp.where(tail_diagonal, edge_real[:, 1, None, None], real_part)
    imag_part = jnp.where(lower_corner, corner_imag[:, 0, None, None], imag_part)
    imag_part = jnp.where(upper_corner, corner_imag[:, 1, None, None], imag_part)
    imag_part = jnp.where(head_diagonal, edge_imag[:, 0, None, None], imag_part)
    imag_part = jnp.where(tail_diagonal, edge_imag[:, 1, None, None], imag_part)
    return jnp.stack([real_part, imag_part]).reshape(2, groups * length, length)


def draw_row_inverse(key, part):
    return draw_inverse(jax.random.fold_in(key, 11), NY // CY, CY)


def draw_column_inverse(key, part):
    return draw_inverse(jax.random.fold_in(key, 23), NZ // CZ, CZ)


def draw_shell_blocks(key, part):
    devices = NZ // CZ * (NY // CY)
    subkeys = jax.random.split(jax.random.fold_in(key, 31), devices)
    chosen = jax.vmap(lambda member_key: jax.random.permutation(member_key, BPD)[:SHELL_DEV])(subkeys)
    return chosen.reshape(NZ // CZ, NY // CY, SHELL_DEV).astype(jnp.int32)


def steps_of(stream_key, dims, cuts, smallest, largest):
    loudness = 1.0
    for dim, blocks in cuts:
        heights = jax.random.uniform(jax.random.fold_in(jax.random.fold_in(stream_key, 6), dim), (blocks,), jnp.float32, smallest / len(cuts), largest / len(cuts))
        loudness = loudness * jnp.repeat(jnp.exp(heights), dims[dim] // blocks).reshape((-1,) + (1,) * (len(dims) - 1 - dim))
    return loudness


def deal_out(stream_key, own, number, rows, amount, top, most, lean):
    ranking = jax.random.permutation(stream_key, amount)
    packed, common = portions_of(amount, rows * top, most, lean, True), portions_of(amount, rows * top, most, lean, False)
    places = jnp.arange(amount)

    def named(sizes, rotation):
        used = int((sizes > 0).sum())
        fixed = max(1, used // 4)
        moved = fixed + (places - fixed + rotation * (used - fixed)) % max(1, amount - fixed)
        return jnp.zeros((amount,), jnp.int32).at[ranking[jnp.where(places < fixed, places, moved)]].set(jnp.asarray(sizes, jnp.int32))

    sizes = jnp.where(number % 4 == 0, named(packed, number // 4), named(common, number - number // 4 - 1))
    mixed = jax.random.permutation(jax.random.fold_in(own, 3), amount)
    source_of, sink = mixed[0:amount // 2 * 2:2], mixed[1:amount // 2 * 2:2]
    room = jnp.minimum(sizes[source_of] - 1, most - sizes[sink]) // 2
    room = jnp.where((source_of == ranking[0]) | (sink == ranking[0]) | (sizes[sink] == 0), 0, jnp.maximum(room, 0))
    moved = jax.random.randint(jax.random.fold_in(own, 4), (amount // 2,), 0, 1 << 20) % (room + 1)
    sizes = sizes.at[source_of].add(-moved).at[sink].add(moved)
    members = jnp.searchsorted(jnp.cumsum(sizes), jnp.arange(rows * top), side="right").astype(jnp.int32)
    table = members.reshape(top, rows).T
    table = table[jax.random.permutation(jax.random.fold_in(own, 1), rows)]
    rotation = jax.random.randint(jax.random.fold_in(own, 2), (rows, 1), 0, top)
    return jnp.take_along_axis(table, (jnp.arange(top)[None, :] + rotation) % top, axis=1)


def portions_of(amount, total, reach, lean, full):
    portions = [(1 << 20) // math.isqrt(grade ** lean) + 1 for grade in range(1, amount + 1)]
    largest = reach if full else min(reach, max(-(-total // amount), total * portions[0] // sum(portions)))
    least = 1 if total - largest >= amount - 1 else 0
    holding, rest = [largest] + [least] * (amount - 1), total - largest - least * (amount - 1)
    while rest > 0:
        candidates = [i for i in range(1, amount) if holding[i] < largest] or [i for i in range(1, amount) if holding[i] < reach]
        pool, remaining = sum([portions[i] for i in candidates]), rest
        for i in candidates:
            more = min(reach - holding[i], max(1, remaining * portions[i] // pool), rest)
            holding[i] = holding[i] + more
            rest = rest - more
    return np.array(holding)


def centred(own_key, extent, scale, reach, shards=(), held_as=jnp.bfloat16):
    entries = jax.random.normal(own_key, extent, jnp.float32) * scale
    if len(shards) > 0:
        entries = steps_of(own_key, extent, shards, -0.22, 0.18) * entries
    return jnp.clip(entries, min=-reach, max=reach).astype(held_as)


def setup_inputs(seed: int = 0) -> dict:
    splits = jax.random.split(jax.random.key(seed), 9)
    wavefunction = centred(splits[0], (2, NX, NY, NZ), 1.0, 6.0, ((2, 32), (3, 8)), jnp.float32)
    absorber = jnp.clip(jnp.exp(math.log(1.5) - 3.4011974 * jax.random.uniform(splits[1], (NX, NY, NZ), jnp.float32) ** steps_of(splits[1], (NX, NY, NZ), ((1, 32), (2, 8)), -0.2, 0.2)), 0.05, 1.5)
    row_inverse = draw_row_inverse(jax.random.fold_in(splits[8], 71), 0)
    column_inverse = draw_column_inverse(jax.random.fold_in(splits[8], 71), 0)
    link_terms = jnp.clip(jax.random.uniform(splits[4], (2, 2, 2), jnp.float32, 0.65, 0.7), 0.65, 0.7)
    shell_blocks = draw_shell_blocks(jax.random.fold_in(splits[8], 71), 0)
    owner_map_keys = jax.random.split(jax.random.fold_in(splits[6], 1), N_GZ * N_GY * SHELL_DEV // SHELL_DEV)
    owner_map_turns = jax.random.permutation(jax.random.fold_in(splits[6], 3), N_GZ * N_GY * SHELL_DEV // SHELL_DEV)
    owner_map = jax.vmap(lambda own, number: deal_out(jax.random.fold_in(splits[6], 2), own, number, SHELL_DEV, N_GY, 1, CAP, 2))(owner_map_keys, owner_map_turns).reshape((N_GZ, N_GY, SHELL_DEV, 1))
    volkov_phase = jnp.clip(jax.random.uniform(splits[7], (KY, KZ), jnp.float32, -3.140625, 3.140625), -3.140625, 3.140625)
    return {"wavefunction": wavefunction, "absorber": absorber, "row_inverse": row_inverse, "column_inverse": column_inverse, "link_terms": link_terms, "shell_blocks": shell_blocks, "owner_map": owner_map, "volkov_phase": volkov_phase}


precise = lax.Precision.HIGHEST

def complex_mul(former, latter):
    return (former[0] * latter[0] - former[1] * latter[1], former[0] * latter[1] + former[1] * latter[0])

def complex_div(former, latter):
    modulus = latter[0] * latter[0] + latter[1] * latter[1]
    return ((former[0] * latter[0] + former[1] * latter[1]) / modulus, (former[1] * latter[0] - former[0] * latter[1]) / modulus)

def complex_add(former, latter):
    return (former[0] + latter[0], former[1] + latter[1])

def complex_sub(former, latter):
    return (former[0] - latter[0], former[1] - latter[1])

def complex_einsum(pattern, former, latter):
    real_part = jnp.einsum(pattern, former[0], latter[0], precision=precise) - jnp.einsum(pattern, former[1], latter[1], precision=precise)
    imag_part = jnp.einsum(pattern, former[0], latter[1], precision=precise) + jnp.einsum(pattern, former[1], latter[0], precision=precise)
    return (real_part, imag_part)

def phase_table(positions, count):
    wavenum = jnp.arange(count, dtype=jnp.int32)
    turns = positions[..., None] * wavenum % count
    parity = (positions[..., None] % 2).astype(jnp.float32)
    phases = 2.0 * math.pi / count * turns.astype(jnp.float32) - math.pi * parity
    return (jnp.cos(phases), -jnp.sin(phases))

def edge_terms(inverse, prev_link, next_link):
    length = inverse[0].shape[-1]
    left_spike = complex_mul(prev_link, (inverse[0][..., 0], inverse[1][..., 0]))
    right_spike = complex_mul(next_link, (inverse[0][..., length - 1], inverse[1][..., length - 1]))
    edges = ((left_spike[0][..., 0], left_spike[1][..., 0]), (left_spike[0][..., length - 1], left_spike[1][..., length - 1]), (right_spike[0][..., 0], right_spike[1][..., 0]), (right_spike[0][..., length - 1], right_spike[1][..., length - 1]))
    return (left_spike, right_spike, edges)

def chain_local(edges, head_part, tail_part):
    unity = (jnp.ones((), jnp.float32), jnp.zeros((), jnp.float32))

    def forward(carry, inputs):
        coupling, carried = carry
        spikes, head_now, tail_now = inputs
        pivot_value = complex_sub(unity, complex_mul(spikes[0], coupling))
        gain_term = complex_div(spikes[1], pivot_value)
        coupling_next = complex_add(spikes[3], complex_mul(gain_term, complex_mul(spikes[2], coupling)))
        carried_next = complex_add(complex_mul(gain_term, carried), complex_add(tail_now, complex_mul(complex_mul(gain_term, coupling), head_now)))
        return ((coupling_next, carried_next), (coupling, carried, pivot_value))
    zero_lines = (jnp.zeros_like(head_part[0][0]), jnp.zeros_like(head_part[0][0]))
    initial = ((jnp.zeros((), jnp.float32), jnp.zeros((), jnp.float32)), zero_lines)
    final_state, (coupling_prev, carried_prev, pivots) = lax.scan(forward, initial, (edges, head_part, tail_part))

    def backward(head_next, inputs):
        spikes, head_now, carried_now, coupling_now, pivot_value = inputs
        offset = complex_div(complex_add(head_now, complex_mul(spikes[0], carried_now)), pivot_value)
        factor = complex_div(spikes[2], pivot_value)
        head_value = complex_add(offset, complex_mul(factor, head_next))
        left_value = complex_add(carried_now, complex_mul(coupling_now, head_value))
        return (head_value, (left_value, head_next))
    final_head, (left_values, right_values) = lax.scan(backward, zero_lines, (edges, head_part, carried_prev, coupling_prev, pivots), reverse=True)
    return (left_values, right_values)

def reference(wavefunction, absorber, row_inverse, column_inverse, link_terms, shell_blocks, owner_map, volkov_phase):
    row_count = NY // CY
    column_count = NZ // CZ
    row_groups = (row_inverse[0].reshape(row_count, CY, CY), row_inverse[1].reshape(row_count, CY, CY))
    column_groups = (column_inverse[0].reshape(column_count, CZ, CZ), column_inverse[1].reshape(column_count, CZ, CZ))
    row_left, row_right, row_edges = edge_terms(row_groups, (link_terms[0, 0, 0], link_terms[0, 0, 1]), (link_terms[0, 1, 0], link_terms[0, 1, 1]))
    column_left, column_right, column_edges = edge_terms(column_groups, (link_terms[1, 0, 0], link_terms[1, 0, 1]), (link_terms[1, 1, 0], link_terms[1, 1, 1]))
    weight_norm = 1.0 / math.sqrt(CY * CZ)
    volkov = (jnp.cos(volkov_phase), jnp.sin(volkov_phase))

    def plane_step(inputs):
        field, damping = inputs
        blocks = (field[0].reshape(row_count, CY, NZ), field[1].reshape(row_count, CY, NZ))
        solved = complex_einsum('jab,jbz->jaz', row_groups, blocks)
        head_part = (solved[0][:, 0], solved[1][:, 0])
        tail_part = (solved[0][:, CY - 1], solved[1][:, CY - 1])
        left_value, right_value = chain_local(row_edges, head_part, tail_part)
        lifted = complex_add(solved, complex_add(complex_mul((row_left[0][:, :, None], row_left[1][:, :, None]), (left_value[0][:, None, :], left_value[1][:, None, :])), complex_mul((row_right[0][:, :, None], row_right[1][:, :, None]), (right_value[0][:, None, :], right_value[1][:, None, :]))))
        field_y = (lifted[0].reshape(NY, column_count, CZ), lifted[1].reshape(NY, column_count, CZ))
        solved_z = complex_einsum('jab,yjb->yja', column_groups, field_y)
        head_z = (solved_z[0][:, :, 0].T, solved_z[1][:, :, 0].T)
        tail_z = (solved_z[0][:, :, CZ - 1].T, solved_z[1][:, :, CZ - 1].T)
        left_z, right_z = chain_local(column_edges, head_z, tail_z)
        lifted_z = complex_add(solved_z, complex_add(complex_mul((column_left[0][None], column_left[1][None]), (left_z[0].T[:, :, None], left_z[1].T[:, :, None])), complex_mul((column_right[0][None], column_right[1][None]), (right_z[0].T[:, :, None], right_z[1].T[:, :, None]))))
        field_z = (lifted_z[0].reshape(NY, NZ), lifted_z[1].reshape(NY, NZ))
        kept = jnp.exp(-damping)
        damped = (field_z[0] * kept, field_z[1] * kept)
        lost_stack = jnp.stack([field_z[0] - damped[0], field_z[1] - damped[1]])

        def group_spectrum(position):
            pieces = lax.dynamic_slice_in_dim(lost_stack, (position * CZ).astype(jnp.int32), CZ, axis=2)
            blocks_all = pieces.reshape(2, row_count, BPD, BY, CZ)
            chosen_ids = shell_blocks[position]
            picked = blocks_all[:, jnp.arange(row_count, dtype=jnp.int32)[:, None], chosen_ids]
            z_table = phase_table(position * CZ + jnp.arange(CZ, dtype=jnp.int32), KZ)
            moved = complex_einsum('gmbz,zq->gmbq', (picked[0], picked[1]), z_table)
            rows_y = jnp.arange(row_count, dtype=jnp.int32)[:, None, None] * CY + chosen_ids[:, :, None] * BY + jnp.arange(BY, dtype=jnp.int32)[None, None, :]
            y_table = phase_table(rows_y, KY)
            terms = complex_einsum('gmbk,gmbq->gmkq', y_table, moved)
            targets = owner_map[position, :, :, 0].reshape(-1)
            summed = tuple((jax.ops.segment_sum(member.reshape(row_count * SHELL_DEV, KY, KZ), targets, num_segments=row_count) for member in terms))
            phased = complex_mul(volkov, summed)
            return jnp.stack([phased[0], phased[1]]) * weight_norm
        spectra = lax.map(group_spectrum, jnp.arange(column_count, dtype=jnp.int32))
        return (jnp.stack([damped[0], damped[1]]), spectra)
    planes_out, spectra = lax.map(plane_step, (jnp.moveaxis(wavefunction, 1, 0), absorber))
    damped_all = jnp.moveaxis(planes_out, 0, 1)
    spectrum = spectra.transpose(2, 3, 0, 1, 4, 5).reshape(2, row_count * NX, column_count * KY, KZ)
    return (damped_all, spectrum)
```

```python
import math

import jax
import jax.numpy as jnp
import numpy as np
from jax import lax
from jax.experimental import pallas as pl
from jax.experimental.pallas import tpu as pltpu
from jax.sharding import PartitionSpec as P

MESH = pl.DeviceIdType.MESH
BF = jnp.bfloat16
F32 = jnp.float32

NX = 8
CY = 128
CZ = 256
K = 128
BY = 2
CAP = 4
NG = 32
NC = 8
UNITS = 16
CHUNKS = 2
PER = NX // CHUNKS


def split(value):
    high = value.astype(BF)
    return high, (value - high.astype(F32)).astype(BF)


NN = (((1,), (0,)), ((), ()))
NT = (((1,), (1,)), ((), ()))


def dot(a, b, dims=NN):
    return lax.dot_general(a, b, dims, preferred_element_type=F32)


def dot3(ah, al, bh, bl, dims=NN):
    return dot(ah, bh, dims) + dot(ah, bl, dims) + dot(al, bh, dims)


def cmul(a, b):
    return (a[0] * b[0] - a[1] * b[1], a[0] * b[1] + a[1] * b[0])


def cadd(a, b):
    return (a[0] + b[0], a[1] + b[1])


def chain(count, stride, edges_of, keep, result):
    lane = lax.broadcasted_iota(jnp.int32, (1, 128), 1)

    def units(j):
        one = lambda i: (lane == stride * j + i).astype(F32)
        return (one(0), one(1)), (one(2), one(3))

    def forward(j, carry):
        coupling, carried = (carry[0], carry[1]), (carry[2], carry[3])
        lead_left, tail_left, lead_right, tail_right = edges_of(j)
        head, tail = units(j)
        step = cmul(lead_left, coupling)
        pivot = (1.0 - step[0], -step[1])
        modulus = pivot[0] * pivot[0] + pivot[1] * pivot[1]
        inverse = (pivot[0] / modulus, -pivot[1] / modulus)
        gain = cmul(tail_left, inverse)
        keep[j, 0:1, :] = coupling[0]
        keep[j, 1:2, :] = coupling[1]
        keep[j, 2:3, :] = carried[0]
        keep[j, 3:4, :] = carried[1]
        keep[j, 4:5, :] = inverse[0]
        keep[j, 5:6, :] = inverse[1]
        after = cadd(tail_right, cmul(gain, cmul(lead_right, coupling)))
        held = cadd(cmul(gain, carried), cadd(tail, cmul(cmul(gain, coupling), head)))
        return (after[0], after[1], held[0], held[1])

    zero = jnp.zeros((1, 128), F32)
    lax.fori_loop(0, count, forward, (zero, zero, zero, zero))

    def backward(k, carry):
        j = count - 1 - k
        following = (carry[0], carry[1])
        lead_left, _, lead_right, _ = edges_of(j)
        head, _ = units(j)
        coupling = (keep[j, 0:1, :], keep[j, 1:2, :])
        carried = (keep[j, 2:3, :], keep[j, 3:4, :])
        inverse = (keep[j, 4:5, :], keep[j, 5:6, :])
        offset = cmul(cadd(head, cmul(lead_left, carried)), inverse)
        value = cadd(offset, cmul(cmul(lead_right, inverse), following))
        left = cadd(carried, cmul(coupling, value))
        result[j, 0:1, :] = left[0]
        result[j, 1:2, :] = left[1]
        result[j, 2:3, :] = following[0]
        result[j, 3:4, :] = following[1]
        return value

    lax.fori_loop(0, count, backward, (zero, zero))


def kernel(
    links,
    slots,
    wave_hbm,
    absorber_hbm,
    row_hbm,
    column_hbm,
    place_row,
    volkov,
    etab,
    ftab,
    damped_hbm,
    spectrum_hbm,
    wave,
    absorber,
    row,
    column,
    top,
    bottom,
    yemb,
    yedge32,
    yedge,
    spikes,
    psi,
    edge_tile,
    edges,
    heads,
    gathered,
    keep,
    response,
    flat_a,
    flat_v,
    values_out,
    values_in,
    solved,
    field,
    zemb,
    zedge32,
    zedge,
    zheads,
    zall,
    zkeep,
    zresponse,
    square,
    zspike,
    zfix,
    solved_z,
    damped,
    fold,
    blocks,
    outgoing,
    incoming,
    ytab,
    spectrum,
    load_sem,
    store_sem,
    edge_sem,
    head_sem,
    value_sem,
    z_sem,
    block_send,
    block_recv,
):
    me = lax.axis_index("gy")
    mez = lax.axis_index("gz")
    half = me // UNITS
    base = half * UNITS
    unit = me - base

    def load(number, source, target):
        copy = pltpu.make_async_copy(source, target, load_sem.at[number])
        copy.start()
        return copy

    row_load = load(0, row_hbm, row)
    wave_load = load(1, wave_hbm, wave)
    column_load = load(2, column_hbm.at[:, mez], column)
    top_load = load(3, column_hbm.at[:, :, pl.ds(0, 8), :], top)
    bottom_load = load(4, column_hbm.at[:, :, pl.ds(CZ - 8, 8), :], bottom)
    absorber_load = load(5, absorber_hbm, absorber)

    barrier = pltpu.get_barrier_semaphore()

    def greet(s, carry):
        pl.semaphore_signal(
            barrier, inc=1, device_id={"gy": lax.rem(me + s, NG)}, device_id_type=MESH
        )
        return carry

    def greet_z(s, carry):
        pl.semaphore_signal(
            barrier, inc=1, device_id={"gz": lax.rem(mez + s, NC)}, device_id_type=MESH
        )
        return carry

    lax.fori_loop(1, NG, greet, 0)
    lax.fori_loop(1, NC, greet_z, 0)

    row_load.wait()
    yr, yi = row[0], row[1]
    for part, (value, sign) in enumerate(((yr, 1.0), (yi, 1.0))):
        high, low = split(value)
        for n, piece in enumerate((high, low)):
            if part == 0:
                yemb[n, 0:CY, 0:CY] = piece
                yemb[n, CY:, CY:] = piece
            else:
                yemb[n, 0:CY, CY:] = -piece
                yemb[n, CY:, 0:CY] = piece
    yedge32[...] = jnp.zeros_like(yedge32)
    for n, r in enumerate((0, CY - 1)):
        yedge32[2 * n : 2 * n + 1, 0:CY] = row[0, r : r + 1, :]
        yedge32[2 * n : 2 * n + 1, CY:] = -row[1, r : r + 1, :]
        yedge32[2 * n + 1 : 2 * n + 2, 0:CY] = row[1, r : r + 1, :]
        yedge32[2 * n + 1 : 2 * n + 2, CY:] = row[0, r : r + 1, :]
    high, low = split(yedge32[...])
    yedge[0], yedge[1] = high, low

    for side, place in enumerate((0, CY - 1)):
        link = (links[2 * side], links[2 * side + 1])
        spike = cmul(link, (yr[:, place : place + 1], yi[:, place : place + 1]))
        for part in range(2):
            spikes[2 * side + part] = jnp.broadcast_to(spike[part], (CY, 128))
            for n, r in enumerate((0, CY - 1)):
                edge_tile[4 * side + 2 * n + part : 4 * side + 2 * n + part + 1, :] = (
                    spikes[2 * side + part, r : r + 1, :]
                )

    pl.semaphore_wait(barrier, NG - 1 + NC - 1)

    def send_edges(s, carry):
        pltpu.make_async_remote_copy(
            src_ref=edge_tile,
            dst_ref=edges.at[me],
            send_sem=edge_sem.at[0],
            recv_sem=edge_sem.at[1],
            device_id={"gy": lax.rem(me + s, NG)},
            device_id_type=MESH,
        ).start()
        return carry

    lax.fori_loop(1, NG, send_edges, 0)
    edges[me] = edge_tile[...]

    wave_load.wait()

    def head_step(x, carry):
        value = jnp.concatenate([wave[0, x], wave[1, x]], axis=0)
        high, low = split(value)
        psi[0, x], psi[1, x] = high, low
        found = dot3(yedge[0], yedge[1], high, low)
        heads[2 * x] = found[0:4, 0:128]
        heads[2 * x + 1] = found[0:4, 128:256]
        return carry

    lax.fori_loop(0, NX, head_step, 0, unroll=True)

    def send_heads(s, carry):
        peer = lax.rem(me + s, NG)
        pltpu.make_async_remote_copy(
            src_ref=heads.at[lax.rem(peer, UNITS)],
            dst_ref=gathered.at[me],
            send_sem=head_sem.at[0],
            recv_sem=head_sem.at[1],
            device_id={"gy": peer},
            device_id_type=MESH,
        ).start()
        return carry

    lax.fori_loop(1, NG, send_heads, 0)
    gathered[me] = heads[unit]

    pltpu.make_async_copy(edges.at[pl.ds(0, NG - 1)], edges.at[pl.ds(0, NG - 1)], edge_sem.at[1]).wait()

    def row_edges(j):
        return [
            (edges[j, r : r + 1, :], edges[j, r + 1 : r + 2, :]) for r in (0, 2, 4, 6)
        ]

    chain(NG, 4, row_edges, keep, response)
    for j in range(NG):
        flat_a[4 * j : 4 * j + 4, :] = response[j]

    def solve_step(x, carry):
        solved[x] = dot3(yemb[0], yemb[1], psi[0, x], psi[1, x])
        return carry

    lax.fori_loop(0, NX, solve_step, 0, unroll=True)

    pltpu.make_async_copy(
        gathered.at[pl.ds(0, NG - 1)], gathered.at[pl.ds(0, NG - 1)], head_sem.at[1]
    ).wait()
    for j in range(NG):
        flat_v[4 * j : 4 * j + 4, :] = gathered[j]
    ah, al = split(flat_a[...])
    vh, vl = split(flat_v[...])
    found = dot3(ah, al, vh, vl)
    for j in range(NG):
        values_out[j] = found[4 * j : 4 * j + 4, :]

    def send_values(s, carry):
        peer = base + lax.rem(unit + s, UNITS)
        pltpu.make_async_remote_copy(
            src_ref=values_out.at[peer],
            dst_ref=values_in.at[unit],
            send_sem=value_sem.at[0],
            recv_sem=value_sem.at[1],
            device_id={"gy": peer},
            device_id_type=MESH,
        ).start()
        return carry

    lax.fori_loop(1, UNITS, send_values, 0)
    values_in[unit] = values_out[me]

    column_load.wait()
    for part in range(2):
        for n, piece in enumerate(split(column[part])):
            if part == 0:
                zemb[n, 0:CZ, 0:CZ] = piece
                zemb[n, CZ:, CZ:] = piece
            else:
                zemb[n, 0:CZ, CZ:] = -piece
                zemb[n, CZ:, 0:CZ] = piece
    zedge32[...] = jnp.zeros_like(zedge32)
    for n, r in enumerate((0, CZ - 1)):
        zedge32[2 * n : 2 * n + 1, 0:CZ] = column[0, r : r + 1, :]
        zedge32[2 * n : 2 * n + 1, CZ:] = -column[1, r : r + 1, :]
        zedge32[2 * n + 1 : 2 * n + 2, 0:CZ] = column[1, r : r + 1, :]
        zedge32[2 * n + 1 : 2 * n + 2, CZ:] = column[0, r : r + 1, :]
    high, low = split(zedge32[...])
    zedge[0], zedge[1] = high, low

    for side in range(2):
        link = (links[4 + 2 * side], links[5 + 2 * side])
        lines = []
        for part in range(2):
            pieces = []
            for a in range(2):
                turned = jnp.transpose(
                    column[part, 128 * a : 128 * a + 128, 128 * side : 128 * side + 128]
                )
                pieces.append(turned[0:1, :] if side == 0 else turned[127:128, :])
            lines.append(jnp.concatenate(pieces, axis=1))
        spike = cmul(link, (lines[0], lines[1]))
        zspike[2 * side : 2 * side + 1, 0:CZ] = spike[0]
        zspike[2 * side : 2 * side + 1, CZ:] = spike[1]
        zspike[2 * side + 1 : 2 * side + 2, 0:CZ] = -spike[1]
        zspike[2 * side + 1 : 2 * side + 2, CZ:] = spike[0]

    top_load.wait()
    bottom_load.wait()

    def column_edges(c):
        out = []
        for side, place in enumerate((0, CZ - 1)):
            link = (links[4 + 2 * side], links[5 + 2 * side])
            for table, r in ((top, 0), (bottom, 7)):
                value = tuple(
                    jnp.broadcast_to(table[part, c, r : r + 1, place : place + 1], (1, 128))
                    for part in range(2)
                )
                out.append(cmul(link, value))
        return out

    chain(NC, 8, column_edges, zkeep, zresponse)
    square[...] = jnp.zeros_like(square)
    square[0:4, :] = zresponse[mez]
    turned = jnp.transpose(square[...])
    for h in range(2):
        total = jnp.zeros((64, 2 * CZ), F32)
        for i in range(4):
            total = total + turned[0:64, i : i + 1] * zspike[i : i + 1, :]
        if h == 0:
            held = total
        else:
            held = pltpu.roll(held, 4, 0)
        high, low = split(held)
        zfix[h, 0:64, :] = high
        zfix[h, 64:128, :] = high
        zfix[h, 128:192, :] = low
        zfix[h, 192:256, :] = low

    wanted = lax.broadcasted_iota(jnp.int32, (2 * K, 16 * NG), 0)
    onehot = (wanted == place_row[...]).astype(F32).astype(BF)
    for n in range(2):
        ytab[n] = dot(etab[n], onehot).astype(BF)

    pltpu.make_async_copy(
        values_in.at[pl.ds(0, UNITS - 1)], values_in.at[pl.ds(0, UNITS - 1)], value_sem.at[1]
    ).wait()

    def field_step(x, carry):
        for h in range(2):
            v = values_in[2 * x + h]
            lre, lim, rre, rim = (v[i : i + 1, :] for i in range(4))
            re = solved[x, 0:CY, 128 * h : 128 * h + 128]
            im = solved[x, CY:, 128 * h : 128 * h + 128]
            re = re + (spikes[0] * lre - spikes[1] * lim) + (spikes[2] * rre - spikes[3] * rim)
            im = im + (spikes[0] * lim + spikes[1] * lre) + (spikes[2] * rim + spikes[3] * rre)
            for part, value in enumerate((re, im)):
                high, low = split(value)
                at = CZ * part + 128 * h
                field[0, x, :, at : at + 128] = high
                field[1, x, :, at : at + 128] = low
        return carry

    lax.fori_loop(0, NX, field_step, 0)

    for x in range(NX):
        found = dot3(zedge[0], zedge[1], field[0, x], field[1, x], NT)
        at = 4 * (x // 4)
        zheads[at : at + 4, 128 * (x % 4) : 128 * (x % 4) + 128] = found[0:4, :]

    def send_zheads(s, carry):
        pltpu.make_async_remote_copy(
            src_ref=zheads,
            dst_ref=zall.at[mez],
            send_sem=z_sem.at[0],
            recv_sem=z_sem.at[1],
            device_id={"gz": lax.rem(mez + s, NC)},
            device_id_type=MESH,
        ).start()
        return carry

    lax.fori_loop(1, NC, send_zheads, 0)
    zall[mez] = zheads[...]

    def solve_z(x, carry):
        solved_z[x] = dot3(field[0, x], field[1, x], zemb[0], zemb[1], NT)
        return carry

    lax.fori_loop(0, NX, solve_z, 0, unroll=True)
    absorber_load.wait()

    pltpu.make_async_copy(
        zall.at[pl.ds(0, NC - 1)], zall.at[pl.ds(0, NC - 1)], z_sem.at[1]
    ).wait()

    for part in range(CHUNKS):
        for x in range(PER * part, PER * part + PER):
            lanes = 128 * (x % 4)
            g = zall[:, :, lanes : lanes + 128].reshape(8 * NC, 128)
            high = g.astype(BF).astype(F32)
            turned = jnp.transpose(jnp.concatenate([high, g - high], axis=0)).astype(BF)
            fix = dot(jnp.concatenate([turned, turned], axis=1), zfix[x // 4])
            kept = jnp.exp(-absorber[x])
            for c in range(2):
                value = solved_z[x, :, CZ * c : CZ * c + CZ] + fix[:, CZ * c : CZ * c + CZ]
                left = value * kept
                damped[c, x] = left
                lost = value - left
                fold[c] = lost[:, 0:128] + lost[:, 128:256]
                for b in range(BY):
                    blocks[x, pl.ds(2 * c + b, K // BY, stride=4), :] = fold[
                        c, pl.ds(b, K // BY, stride=BY), :
                    ]

        def pack(o, carry):
            for l in range(CAP):
                at = slots[CAP * o + l]
                for x in range(PER * part, PER * part + PER):
                    outgoing[x, o, 4 * l : 4 * l + 4, :] = blocks[x, pl.ds(at, 4), :]
            return carry

        lax.fori_loop(0, NG, pack, 0)

        def send_blocks(s, carry):
            peer = lax.rem(me + s, NG)
            pltpu.make_async_remote_copy(
                src_ref=outgoing.at[pl.ds(PER * part, PER), peer],
                dst_ref=incoming.at[pl.ds(PER * part, PER), me],
                send_sem=block_send.at[part],
                recv_sem=block_recv.at[part],
                device_id={"gy": peer},
                device_id_type=MESH,
            ).start()
            return carry

        lax.fori_loop(1, NG, send_blocks, 0)
        for x in range(PER * part, PER * part + PER):
            incoming[x, me] = outgoing[x, me]

    damped_store = pltpu.make_async_copy(damped, damped_hbm, store_sem.at[0])
    damped_store.start()
    norm = 1.0 / math.sqrt(CY * CZ)

    stores = []
    for part in range(CHUNKS):
        pltpu.make_async_copy(
            incoming.at[pl.ds(PER * part, PER), pl.ds(0, NG - 1)],
            incoming.at[pl.ds(PER * part, PER), pl.ds(0, NG - 1)],
            block_recv.at[part],
        ).wait()
        for x in range(PER * part, PER * part + PER):
            high, low = split(incoming[x].reshape(16 * NG, 128))
            along_y = dot3(ytab[0], ytab[1], high, low)
            high, low = split(jnp.concatenate([along_y[0:K, :], along_y[K:, :]], axis=1))
            both = dot3(high, low, ftab[0], ftab[1])
            re, im = cmul((volkov[0], volkov[1]), (both[:, 0:K], both[:, K:]))
            spectrum[0, x] = re * norm
            spectrum[1, x] = im * norm
        store = pltpu.make_async_copy(
            spectrum.at[:, pl.ds(PER * part, PER)],
            spectrum_hbm.at[:, pl.ds(PER * part, PER)],
            store_sem.at[1 + part],
        )
        store.start()
        stores.append(store)

    def sent(ref, count, sem):
        view = ref.at[pl.ds(0, count)]
        pltpu.make_async_copy(view, view, sem).wait()

    sent(edges, NG - 1, edge_sem.at[0])
    sent(gathered, NG - 1, head_sem.at[0])
    sent(values_in, UNITS - 1, value_sem.at[0])
    sent(zall, NC - 1, z_sem.at[0])
    for part in range(CHUNKS):
        view = outgoing.at[pl.ds(PER * part, PER), pl.ds(0, NG - 1)]
        pltpu.make_async_copy(view, view, block_send.at[part]).wait()
    damped_store.wait()
    for store in stores:
        store.wait()


def phase_tables():
    n, k = np.arange(K)[:, None], np.arange(K)[None, :]
    angle = 2.0 * np.pi / K * ((n * k) % K) - np.pi * (n % 2)
    re, im = np.cos(angle), -np.sin(angle)
    along_y = np.block([[re.T, -im.T], [im.T, re.T]]).astype(np.float32)
    along_z = np.block([[re, im], [-im, re]]).astype(np.float32)
    found = []
    for table in (along_y, along_z):
        high = table.astype(BF)
        found.append(np.stack([high, (table - high.astype(np.float32)).astype(BF)]))
    return found


def body(
    wavefunction,
    absorber,
    row_inverse,
    column_inverse,
    link_terms,
    shell_blocks,
    owner_map,
    volkov_phase,
):
    row_rank = lax.axis_index("gy")
    listed, targets = shell_blocks[0], owner_map[0, :, :, 0]
    count = listed.shape[1]
    places = jnp.arange(count, dtype=jnp.int32)
    earlier = places[:, None] > places[None, :]
    rank = jnp.sum(
        ((targets[:, :, None] == targets[:, None, :]) & earlier[None]).astype(jnp.int32), axis=2
    )
    own = lambda table: lax.dynamic_index_in_dim(table, row_rank, 0, keepdims=False)
    slot = own(targets) * CAP + own(rank)
    numbers = jnp.arange(NG * CAP, dtype=jnp.int32)
    first = 2 * BY * own(listed)[None, :]
    slots = jnp.sum(jnp.where(slot[None, :] == numbers[:, None], first, 0), axis=1)
    hit = (targets == row_rank)[:, None, :] & (
        rank[:, None, :] == jnp.arange(CAP, dtype=jnp.int32)[None, :, None]
    )
    coming = jnp.sum(jnp.where(hit, listed[:, None, :] + 1, 0), axis=2) - 1
    comp = jnp.arange(2, dtype=jnp.int32)[None, None, :, None]
    b = jnp.arange(BY, dtype=jnp.int32)[None, None, None, :]
    block = coming[:, :, None, None]
    place_row = jnp.where(block >= 0, comp * K + BY * block + b, -1).reshape(1, 16 * NG)
    volkov = jnp.stack([jnp.cos(volkov_phase), jnp.sin(volkov_phase)])
    etab, ftab = phase_tables()

    any_space = pl.BlockSpec(memory_space=pl.ANY)
    vmem = pl.BlockSpec(memory_space=pltpu.VMEM)
    smem = pl.BlockSpec(memory_space=pltpu.SMEM)
    V = pltpu.VMEM
    dma = pltpu.SemaphoreType.DMA
    return pl.pallas_call(
        kernel,
        out_shape=(
            jax.ShapeDtypeStruct((2, NX, CY, CZ), F32),
            jax.ShapeDtypeStruct((2, NX, K, K), F32),
        ),
        in_specs=[smem, smem] + [any_space] * 4 + [vmem] * 4,
        out_specs=(any_space, any_space),
        scratch_shapes=[
            V((2, NX, CY, CZ), F32),
            V((NX, CY, CZ), F32),
            V((2, CY, CY), F32),
            V((2, CZ, CZ), F32),
            V((2, NC, 8, CZ), F32),
            V((2, NC, 8, CZ), F32),
            V((2, 2 * CY, 2 * CY), BF),
            V((16, 2 * CY), F32),
            V((2, 16, 2 * CY), BF),
            V((4, CY, 128), F32),
            V((2, NX, 2 * CY, CZ), BF),
            V((8, 128), F32),
            V((NG, 8, 128), F32),
            V((UNITS, 4, 128), F32),
            V((NG, 4, 128), F32),
            V((NG, 8, 128), F32),
            V((NG, 4, 128), F32),
            V((4 * NG, 128), F32),
            V((4 * NG, 128), F32),
            V((NG, 4, 128), F32),
            V((UNITS, 4, 128), F32),
            V((NX, 2 * CY, CZ), F32),
            V((2, NX, CY, 2 * CZ), BF),
            V((2, 2 * CZ, 2 * CZ), BF),
            V((16, 2 * CZ), F32),
            V((2, 16, 2 * CZ), BF),
            V((8, 512), F32),
            V((NC, 8, 512), F32),
            V((NC, 8, 128), F32),
            V((NC, 4, 128), F32),
            V((128, 128), F32),
            V((4, 2 * CZ), F32),
            V((2, 256, 2 * CZ), BF),
            V((NX, CY, 2 * CZ), F32),
            V((2, NX, CY, CZ), F32),
            V((2, CY, 128), F32),
            V((NX, 2 * CY, 128), F32),
            V((NX, NG, 16, 128), F32),
            V((NX, NG, 16, 128), F32),
            V((2, 2 * K, 16 * NG), BF),
            V((2, NX, K, K), F32),
            dma((6,)),
            dma((1 + CHUNKS,)),
            dma((2,)),
            dma((2,)),
            dma((2,)),
            dma((2,)),
            dma((CHUNKS,)),
            dma((CHUNKS,)),
        ],
        compiler_params=pltpu.CompilerParams(
            collective_id=0, has_side_effects=True, vmem_limit_bytes=48 * 1024 * 1024
        ),
    )(
        link_terms.reshape(8),
        slots,
        wavefunction,
        absorber,
        row_inverse,
        column_inverse.reshape(2, NC, CZ, CZ),
        place_row,
        volkov,
        etab,
        ftab,
    )


def solution(mesh):
    placed = (
        P(None, None, "gy", "gz"),
        P(None, "gy", "gz"),
        P(None, "gy", None),
        P(),
        P(),
        P("gz", None, None),
        P("gz", None, None, None),
        P(),
    )
    return jax.shard_map(
        body,
        mesh=mesh,
        in_specs=placed,
        out_specs=(P(None, None, "gy", "gz"), P(None, "gy", "gz", None)),
        check_vma=False,
    )
```

```python
import math

import jax
import jax.numpy as jnp
import numpy as np
from jax import lax
from jax.experimental import pallas as pl
from jax.experimental.pallas import tpu as pltpu
from jax.sharding import PartitionSpec as P

MESH = pl.DeviceIdType.MESH
BF = jnp.bfloat16
F32 = jnp.float32

NX = 8
PAIRS = 4
CY = 128
CZ = 256
K = 128
BY = 2
CAP = 4
SLOT = 2 * BY * CAP
NG = 32
NC = 8
UNITS = 16
PARTS = ((0, 1), (1, 3), (3, 4))


def split(value):
    high = value.astype(BF)
    return high, (value - high.astype(F32)).astype(BF)


NN = (((1,), (0,)), ((), ()))
NT = (((1,), (1,)), ((), ()))


def dot(a, b, dims=NN):
    return lax.dot_general(a, b, dims, preferred_element_type=F32)


def dot3(ah, al, bh, bl, dims=NN):
    return dot(ah, bh, dims) + dot(ah, bl, dims) + dot(al, bh, dims)


def cmul(a, b):
    return (a[0] * b[0] - a[1] * b[1], a[0] * b[1] + a[1] * b[0])


def cadd(a, b):
    return (a[0] + b[0], a[1] + b[1])


def cinv(a):
    modulus = a[0] * a[0] + a[1] * a[1]
    return (a[0] / modulus, -a[1] / modulus)


def chain(count, stride, edges):
    shape = (count, 128)
    place = lax.broadcasted_iota(jnp.int32, shape, 0)
    lane = lax.broadcasted_iota(jnp.int32, shape, 1) - stride * place
    one = jnp.ones(shape, F32)
    zero = jnp.zeros(shape, F32)
    head = ((lane == 0).astype(F32), (lane == 1).astype(F32))
    tail = ((lane == 2).astype(F32), (lane == 3).astype(F32))
    lead_left, tail_left, lead_right, tail_right = edges

    def shifted(value, by, fill):
        if by > 0:
            return jnp.where(place >= by, pltpu.roll(value, by, 0), fill)
        return jnp.where(place < count + by, pltpu.roll(value, count + by, 0), fill)

    def moved(value, by, fill):
        return (shifted(value[0], by, fill), shifted(value[1], by, zero))

    a, b = cmul(tail_left, lead_right), cmul(tail_right, lead_left)
    m = [(a[0] - b[0], a[1] - b[1]), tail_right, (-lead_left[0], -lead_left[1]), (one, zero)]
    by = 1
    while by < count:
        q = [moved(m[0], by, one), moved(m[1], by, zero), moved(m[2], by, zero), moved(m[3], by, one)]
        m = [
            cadd(cmul(m[0], q[0]), cmul(m[1], q[2])),
            cadd(cmul(m[0], q[1]), cmul(m[1], q[3])),
            cadd(cmul(m[2], q[0]), cmul(m[3], q[2])),
            cadd(cmul(m[2], q[1]), cmul(m[3], q[3])),
        ]
        by *= 2
    coupling = cmul(moved(m[1], 1, zero), cinv(moved(m[3], 1, one)))

    def affine(factor, addend, sign):
        by = 1
        while by < count:
            before = (moved(factor, sign * by, one), moved(addend, sign * by, zero))
            addend = cadd(cmul(factor, before[1]), addend)
            factor = cmul(factor, before[0])
            by *= 2
        return addend

    step = cmul(lead_left, coupling)
    inverse = cinv((1.0 - step[0], -step[1]))
    gain = cmul(tail_left, inverse)
    carried = moved(affine(gain, cadd(tail, cmul(cmul(gain, coupling), head)), 1), 1, zero)
    offset = cmul(cadd(head, cmul(lead_left, carried)), inverse)
    value = affine(cmul(lead_right, inverse), offset, -1)
    return cadd(carried, cmul(coupling, value)), moved(value, -1, zero)


def embed(target, size, real, imag):
    for n, piece in enumerate(split(real)):
        target[n, 0:size, 0:size] = piece
        target[n, size:, size:] = piece
    for n, piece in enumerate(split(imag)):
        target[n, 0:size, size:] = -piece
        target[n, size:, 0:size] = piece


def embed_edges(target, wide, size, source):
    wide[...] = jnp.zeros_like(wide)
    for n, r in enumerate((0, size - 1)):
        wide[2 * n : 2 * n + 1, 0:size] = source[0, r : r + 1, :]
        wide[2 * n : 2 * n + 1, size:] = -source[1, r : r + 1, :]
        wide[2 * n + 1 : 2 * n + 2, 0:size] = source[1, r : r + 1, :]
        wide[2 * n + 1 : 2 * n + 2, size:] = source[0, r : r + 1, :]
    target[0], target[1] = split(wide[...])


def rows_of(block):
    k = lax.broadcasted_iota(jnp.int32, (1, SLOT * NG), 1)
    row = (k // BY) % 2 * K + k % BY
    row = jnp.where(block > 0.5, row.astype(F32) + BY * (block - 1.0), -1.0)
    place = lax.broadcasted_iota(jnp.int32, (2 * K, SLOT * NG), 0).astype(F32)
    return (place == row).astype(F32)


def kernel(
    links,
    wave_hbm,
    absorber_hbm,
    row_hbm,
    column_hbm,
    blocks_hbm,
    owners_hbm,
    phase_hbm,
    tables_hbm,
    damped_hbm,
    spectrum_hbm,
    wave,
    absorber,
    row,
    column,
    top,
    bottom,
    listed,
    owners,
    phase,
    tables,
    yemb,
    ywide,
    yedge,
    spikes,
    psi,
    heads,
    gathered,
    edges,
    flat_a,
    flat_v,
    values_out,
    values_in,
    solved,
    field,
    zemb,
    zwide,
    zedge,
    zheads,
    zall,
    zcorner,
    zresponse,
    square,
    zspike,
    zfix,
    padded,
    pick,
    damped,
    outgoing,
    incoming,
    ytab,
    volkov,
    spectrum,
    load_sem,
    damped_sem,
    spectrum_sem,
    head_sem,
    value_sem,
    z_send,
    z_recv,
    block_send,
    block_recv,
):
    me = lax.axis_index("gy")
    mez = lax.axis_index("gz")
    half = me // UNITS
    base = half * UNITS
    unit = me - base

    barrier = pltpu.get_barrier_semaphore()

    def greet(s, carry):
        pl.semaphore_signal(
            barrier, inc=1, device_id={"gy": lax.rem(me + s, NG)}, device_id_type=MESH
        )
        return carry

    def greet_z(s, carry):
        pl.semaphore_signal(
            barrier, inc=1, device_id={"gz": lax.rem(mez + s, NC)}, device_id_type=MESH
        )
        return carry

    def load(number, source, target):
        copy = pltpu.make_async_copy(source, target, load_sem.at[number])
        copy.start()
        return copy

    row_load = load(0, row_hbm, row)
    wave_load = load(1, wave_hbm, wave)
    lax.fori_loop(1, NG, greet, 0)
    lax.fori_loop(1, NC, greet_z, 0)
    column_load = load(2, column_hbm.at[:, mez], column)
    top_load = load(3, column_hbm.at[:, :, pl.ds(0, 8), :], top)
    bottom_load = load(4, column_hbm.at[:, :, pl.ds(CZ - 8, 8), :], bottom)
    blocks_load = load(5, blocks_hbm, listed)
    owners_load = load(6, owners_hbm, owners)
    absorber_load = load(7, absorber_hbm, absorber)
    tables_load = load(8, tables_hbm, tables)
    phase_load = load(9, phase_hbm, phase)

    row_load.wait()
    embed_edges(yedge, ywide, CY, row)
    lane = lax.broadcasted_iota(jnp.int32, (1, 128), 1)
    edge_row = jnp.zeros((1, 128), F32)
    for side, place in enumerate((0, CY - 1)):
        link = (links[0, side, 0], links[0, side, 1])
        spike = cmul(link, (row[0, :, place : place + 1], row[1, :, place : place + 1]))
        for part in range(2):
            spikes[2 * side + part] = jnp.broadcast_to(spike[part], (CY, 128))
            for n, r in enumerate((0, CY - 1)):
                term = spikes[2 * side + part, r : r + 1, :]
                edge_row = jnp.where(lane == 4 * side + 2 * n + part, term, edge_row)
    for u in range(UNITS):
        heads[u, 4] = edge_row

    wave_load.wait()
    for x in range(NX):
        high, low = split(jnp.concatenate([wave[0, x], wave[1, x]], axis=0))
        psi[0, x], psi[1, x] = high, low
        found = dot3(yedge[0], yedge[1], high, low)
        for h in range(2):
            for i in range(4):
                heads[2 * x + h, i] = found[i : i + 1, 128 * h : 128 * h + 128]

    pl.semaphore_wait(barrier, NG - 1 + NC - 1)

    def send_heads(s, carry):
        peer = lax.rem(me + s, NG)
        pltpu.make_async_remote_copy(
            src_ref=heads.at[lax.rem(peer, UNITS)],
            dst_ref=gathered.at[me],
            send_sem=head_sem.at[0],
            recv_sem=head_sem.at[1],
            device_id={"gy": peer},
            device_id_type=MESH,
        ).start()
        return carry

    lax.fori_loop(1, NG, send_heads, 0)
    gathered[me] = heads[unit]

    embed(yemb, CY, row[0], row[1])
    for x in range(NX):
        solved[x] = dot3(yemb[0], yemb[1], psi[0, x], psi[1, x])

    pltpu.make_async_copy(
        gathered.at[pl.ds(0, NG - 1)], gathered.at[pl.ds(0, NG - 1)], head_sem.at[1]
    ).wait()
    for j in range(NG):
        for i in range(4):
            flat_v[4 * j + i : 4 * j + i + 1, :] = gathered[j, i]
        edges[j : j + 1, :] = gathered[j, 4]
    wide = [jnp.broadcast_to(edges[:, i : i + 1], (NG, 128)) for i in range(8)]
    left, right = chain(NG, 4, [(wide[i], wide[i + 1]) for i in (0, 2, 4, 6)])
    for i, value in enumerate(left + right):
        flat_a[pl.ds(i, NG, stride=4), :] = value
    ah, al = split(flat_a[...])
    vh, vl = split(flat_v[...])
    found = dot3(ah, al, vh, vl)
    for j in range(NG):
        values_out[j] = found[4 * j : 4 * j + 4, :]

    def send_values(s, carry):
        peer = base + lax.rem(unit + s, UNITS)
        pltpu.make_async_remote_copy(
            src_ref=values_out.at[peer],
            dst_ref=values_in.at[unit],
            send_sem=value_sem.at[0],
            recv_sem=value_sem.at[1],
            device_id={"gy": peer},
            device_id_type=MESH,
        ).start()
        return carry

    lax.fori_loop(1, UNITS, send_values, 0)
    values_in[unit] = values_out[me]

    column_load.wait()
    embed(zemb, CZ, column[0], column[1])
    embed_edges(zedge, zwide, CZ, column)
    for side in range(2):
        link = (links[1, side, 0], links[1, side, 1])
        lines = []
        for part in range(2):
            pieces = []
            for a in range(2):
                turned = jnp.transpose(
                    column[part, 128 * a : 128 * a + 128, 128 * side : 128 * side + 128]
                )
                pieces.append(turned[0:1, :] if side == 0 else turned[127:128, :])
            lines.append(jnp.concatenate(pieces, axis=1))
        spike = cmul(link, (lines[0], lines[1]))
        zspike[2 * side : 2 * side + 1, 0:CZ] = spike[0]
        zspike[2 * side : 2 * side + 1, CZ:] = spike[1]
        zspike[2 * side + 1 : 2 * side + 2, 0:CZ] = -spike[1]
        zspike[2 * side + 1 : 2 * side + 2, CZ:] = spike[0]

    top_load.wait()
    bottom_load.wait()
    terms = []
    for side, place in enumerate((0, CZ - 1)):
        link = (links[1, side, 0], links[1, side, 1])
        for table, r in ((top, 0), (bottom, 7)):
            for part in range(2):
                for c in range(NC):
                    lanes = 128 * side
                    zcorner[part, c : c + 1, :] = table[part, c, r : r + 1, lanes : lanes + 128]
            at = place % 128
            value = tuple(
                jnp.broadcast_to(zcorner[part][:, at : at + 1], (NC, 128)) for part in range(2)
            )
            terms.append(cmul(link, value))
    left, right = chain(NC, 8, terms)
    square[...] = jnp.zeros_like(square)
    for i, value in enumerate(left + right):
        zresponse[i] = value
        square[i : i + 1, :] = zresponse[i, pl.ds(mez, 1), :]
    turned = jnp.transpose(square[...])
    held = jnp.zeros((64, 2 * CZ), F32)
    for i in range(4):
        held = held + turned[0:64, i : i + 1] * zspike[i : i + 1, :]
    for h in range(2):
        high, low = split(held if h == 0 else pltpu.roll(held, 4, 0))
        zfix[h, 0:64, :] = high
        zfix[h, 64:128, :] = high
        zfix[h, 128:192, :] = low
        zfix[h, 192:256, :] = low

    blocks_load.wait()
    owners_load.wait()
    padded[...] = jnp.full_like(padded, -1.0)
    count = listed.shape[1]
    padded[0, :, 0:count] = listed[...].astype(F32)
    padded[1, :, 0:count] = owners[...].astype(F32)
    ids, names = (
        jnp.transpose(jnp.broadcast_to(padded[n, pl.ds(me, 1), :], (128, 128))) for n in range(2)
    )
    across = lax.broadcasted_iota(jnp.int32, (128, 128), 1)
    down = lax.broadcasted_iota(jnp.int32, (128, 128), 0)
    same = (names == padded[1, pl.ds(me, 1), :]) & (across < down)
    rank = jnp.sum(same.astype(F32), axis=1, keepdims=True)
    slot = jnp.where(names[:, 0:1] < 0.0, -1.0, CAP * names[:, 0:1] + rank)
    k = lax.broadcasted_iota(jnp.int32, (1, SLOT * NG), 1)
    hit = slot == (k // (2 * BY)).astype(F32)
    block = jnp.sum(jnp.where(hit, ids[:, 0:1] + 1.0, 0.0), axis=0, keepdims=True)
    onehot = rows_of(block)
    for n in range(SLOT * NG // 128):
        for m in range(2):
            pick[128 * n : 128 * n + 128, 128 * m : 128 * m + 128] = jnp.transpose(
                onehot[128 * m : 128 * m + 128, 128 * n : 128 * n + 128]
            ).astype(BF)

    pltpu.make_async_copy(
        values_in.at[pl.ds(0, UNITS - 1)], values_in.at[pl.ds(0, UNITS - 1)], value_sem.at[1]
    ).wait()

    for part, (first, last) in enumerate(PARTS):
        for p in range(first, last):
            for x in (2 * p, 2 * p + 1):
                for h in range(2):
                    v = values_in[2 * x + h]
                    lre, lim, rre, rim = (v[i : i + 1, :] for i in range(4))
                    re = solved[x, 0:CY, 128 * h : 128 * h + 128]
                    im = solved[x, CY:, 128 * h : 128 * h + 128]
                    re = re + (spikes[0] * lre - spikes[1] * lim)
                    re = re + (spikes[2] * rre - spikes[3] * rim)
                    im = im + (spikes[0] * lim + spikes[1] * lre)
                    im = im + (spikes[2] * rim + spikes[3] * rre)
                    for c, value in enumerate((re, im)):
                        high, low = split(value)
                        at = CZ * c + 128 * h
                        field[0, x, :, at : at + 128] = high
                        field[1, x, :, at : at + 128] = low
                found = dot3(zedge[0], zedge[1], field[0, x], field[1, x], NT)
                zheads[p, 4 * (x % 2) : 4 * (x % 2) + 4, :] = found[0:4, :]

        def send_zheads(s, carry):
            pltpu.make_async_remote_copy(
                src_ref=zheads.at[pl.ds(first, last - first)],
                dst_ref=zall.at[mez, pl.ds(first, last - first)],
                send_sem=z_send.at[part],
                recv_sem=z_recv.at[part],
                device_id={"gz": lax.rem(mez + s, NC)},
                device_id_type=MESH,
            ).start()
            return carry

        lax.fori_loop(1, NC, send_zheads, 0)
        for p in range(first, last):
            zall[mez, p] = zheads[p]

    stores = []
    for part, (first, last) in enumerate(PARTS):
        planes = pl.ds(2 * first, 2 * (last - first))
        for x in range(2 * first, 2 * last):
            solved[x, 0:CY, :] = dot3(
                field[0, x], field[1, x], zemb[0, 0:CZ, :], zemb[1, 0:CZ, :], NT
            )
            solved[x, CY:, :] = dot3(
                field[0, x], field[1, x], zemb[0, CZ:, :], zemb[1, CZ:, :], NT
            )
        if part == 0:
            absorber_load.wait()
        view = zall.at[pl.ds(0, NC - 1), pl.ds(first, last - first)]
        pltpu.make_async_copy(view, view, z_recv.at[part]).wait()
        for p in range(first, last):
            g = zall[:, p].reshape(8 * NC, 128)
            high = g.astype(BF).astype(F32)
            turned = jnp.transpose(jnp.concatenate([high, g - high], axis=0)).astype(BF)
            turned = jnp.concatenate([turned, turned], axis=1)
            folded = []
            for x in (2 * p, 2 * p + 1):
                fix = dot(turned, zfix[x % 2])
                kept = jnp.exp(-absorber[x])
                rows = []
                for c in range(2):
                    value = solved[x, CY * c : CY * c + CY, :] + fix[:, CZ * c : CZ * c + CZ]
                    left = value * kept
                    damped[c, x] = left
                    lost = value - left
                    rows.append(lost[:, 0:128] + lost[:, 128:256])
                folded.append(jnp.concatenate(rows, axis=0))
            high, low = split(jnp.concatenate(folded, axis=1))
            chosen = dot(pick[...], high) + dot(pick[...], low)
            for n in range(2):
                outgoing[2 * p + n] = chosen[:, 128 * n : 128 * n + 128].reshape(NG, SLOT, 128)

        def send_blocks(s, carry):
            peer = lax.rem(me + s, NG)
            pltpu.make_async_remote_copy(
                src_ref=outgoing.at[planes, peer],
                dst_ref=incoming.at[planes, me],
                send_sem=block_send.at[part],
                recv_sem=block_recv.at[part],
                device_id={"gy": peer},
                device_id_type=MESH,
            ).start()
            return carry

        lax.fori_loop(1, NG, send_blocks, 0)
        for x in range(2 * first, 2 * last):
            incoming[x, me] = outgoing[x, me]
        store = pltpu.make_async_copy(
            damped.at[:, planes], damped_hbm.at[:, planes], damped_sem.at[part]
        )
        store.start()
        stores.append(store)

    source = lax.broadcasted_iota(jnp.int32, (NG, SLOT * NG), 0)
    mine = (padded[1] == me.astype(F32)).astype(F32)
    rank = dot(mine.astype(BF), (down < across).astype(F32).astype(BF))
    total = jnp.zeros((NG, SLOT * NG), F32)
    for n in range(CAP):
        hit = jnp.where(rank == float(n), mine, 0.0)
        found = jnp.sum(hit * (padded[0] + 1.0), axis=1, keepdims=True)
        total = total + jnp.where((k // (2 * BY)) % CAP == n, found, 0.0)
    total = jnp.where(k // SLOT == source, total, 0.0)
    onehot = rows_of(jnp.sum(total, axis=0, keepdims=True)).astype(BF)
    tables_load.wait()
    for n in range(2):
        ytab[n] = dot(tables[n], onehot).astype(BF)
    phase_load.wait()
    norm = 1.0 / math.sqrt(CY * CZ)
    volkov[0] = jnp.cos(phase[...])
    volkov[1] = jnp.sin(phase[...])

    for part, (first, last) in enumerate(PARTS):
        planes = pl.ds(2 * first, 2 * (last - first))
        view = incoming.at[planes, pl.ds(0, NG - 1)]
        pltpu.make_async_copy(view, view, block_recv.at[part]).wait()
        for p in range(first, last):
            both = [incoming[2 * p + n].reshape(SLOT * NG, 128) for n in range(2)]
            high, low = split(jnp.concatenate(both, axis=1))
            along_y = dot3(ytab[0], ytab[1], high, low)
            lines = [
                jnp.concatenate(
                    [along_y[0:K, 128 * n : 128 * n + 128], along_y[K:, 128 * n : 128 * n + 128]],
                    axis=1,
                )
                for n in range(2)
            ]
            high, low = split(jnp.concatenate(lines, axis=0))
            both = dot3(high, low, tables[2], tables[3])
            for n in range(2):
                value = (both[K * n : K * n + K, 0:K], both[K * n : K * n + K, K:])
                re, im = cmul((volkov[0], volkov[1]), value)
                spectrum[0, 2 * p + n] = re * norm
                spectrum[1, 2 * p + n] = im * norm
        store = pltpu.make_async_copy(
            spectrum.at[:, planes], spectrum_hbm.at[:, planes], spectrum_sem.at[part]
        )
        store.start()
        stores.append(store)

    def sent(view, sem):
        pltpu.make_async_copy(view, view, sem).wait()

    sent(gathered.at[pl.ds(0, NG - 1)], head_sem.at[0])
    sent(values_in.at[pl.ds(0, UNITS - 1)], value_sem.at[0])
    for part, (first, last) in enumerate(PARTS):
        sent(zall.at[pl.ds(0, NC - 1), pl.ds(first, last - first)], z_send.at[part])
        planes = pl.ds(2 * first, 2 * (last - first))
        sent(outgoing.at[planes, pl.ds(0, NG - 1)], block_send.at[part])
    for store in stores:
        store.wait()


def phase_tables():
    n, k = np.arange(K)[:, None], np.arange(K)[None, :]
    angle = 2.0 * np.pi / K * ((n * k) % K) - np.pi * (n % 2)
    re, im = np.cos(angle), -np.sin(angle)
    along_y = np.block([[re.T, -im.T], [im.T, re.T]]).astype(np.float32)
    along_z = np.block([[re, im], [-im, re]]).astype(np.float32)
    found = []
    for table in (along_y, along_z):
        high = table.astype(BF)
        found += [high, (table - high.astype(np.float32)).astype(BF)]
    return np.stack(found)


def body(
    wavefunction,
    absorber,
    row_inverse,
    column_inverse,
    link_terms,
    shell_blocks,
    owner_map,
    volkov_phase,
):
    count = shell_blocks.shape[2]
    any_space = pl.BlockSpec(memory_space=pl.ANY)
    smem = pl.BlockSpec(memory_space=pltpu.SMEM)
    V = pltpu.VMEM
    dma = pltpu.SemaphoreType.DMA
    parts = len(PARTS)
    return pl.pallas_call(
        kernel,
        out_shape=(
            jax.ShapeDtypeStruct((2, NX, CY, CZ), F32),
            jax.ShapeDtypeStruct((2, NX, K, K), F32),
        ),
        in_specs=[smem] + [any_space] * 8,
        out_specs=(any_space, any_space),
        scratch_shapes=[
            V((2, NX, CY, CZ), F32),
            V((NX, CY, CZ), F32),
            V((2, CY, CY), F32),
            V((2, CZ, CZ), F32),
            V((2, NC, 8, CZ), F32),
            V((2, NC, 8, CZ), F32),
            V((NG, count), jnp.int32),
            V((NG, count), jnp.int32),
            V((K, K), F32),
            V((4, 2 * K, 2 * K), BF),
            V((2, 2 * CY, 2 * CY), BF),
            V((16, 2 * CY), F32),
            V((2, 16, 2 * CY), BF),
            V((4, CY, 128), F32),
            V((2, NX, 2 * CY, CZ), BF),
            V((UNITS, 5, 1, 128), F32),
            V((NG, 5, 1, 128), F32),
            V((NG, 128), F32),
            V((4 * NG, 128), F32),
            V((4 * NG, 128), F32),
            V((NG, 4, 128), F32),
            V((UNITS, 4, 128), F32),
            V((NX, 2 * CY, CZ), F32),
            V((2, NX, CY, 2 * CZ), BF),
            V((2, 2 * CZ, 2 * CZ), BF),
            V((16, 2 * CZ), F32),
            V((2, 16, 2 * CZ), BF),
            V((PAIRS, 8, 128), F32),
            V((NC, PAIRS, 8, 128), F32),
            V((2, NC, 128), F32),
            V((4, NC, 128), F32),
            V((128, 128), F32),
            V((4, 2 * CZ), F32),
            V((2, 256, 2 * CZ), BF),
            V((2, NG, 128), F32),
            V((SLOT * NG, 2 * K), BF),
            V((2, NX, CY, CZ), F32),
            V((NX, NG, SLOT, 128), F32),
            V((NX, NG, SLOT, 128), F32),
            V((2, 2 * K, SLOT * NG), BF),
            V((2, K, K), F32),
            V((2, NX, K, K), F32),
            dma((10,)),
            dma((parts,)),
            dma((parts,)),
            dma((2,)),
            dma((2,)),
            dma((parts,)),
            dma((parts,)),
            dma((parts,)),
            dma((parts,)),
        ],
        compiler_params=pltpu.CompilerParams(
            collective_id=0, has_side_effects=True, vmem_limit_bytes=48 * 1024 * 1024
        ),
    )(
        link_terms,
        wavefunction,
        absorber,
        row_inverse,
        column_inverse.reshape(2, NC, CZ, CZ),
        shell_blocks.reshape(NG, count),
        owner_map.reshape(NG, count),
        volkov_phase,
        phase_tables(),
    )


def solution(mesh):
    placed = (
        P(None, None, "gy", "gz"),
        P(None, "gy", "gz"),
        P(None, "gy", None),
        P(),
        P(),
        P("gz", None, None),
        P("gz", None, None, None),
        P(),
    )
    return jax.shard_map(
        body,
        mesh=mesh,
        in_specs=placed,
        out_specs=(P(None, None, "gy", "gz"), P(None, "gy", "gz", None)),
        check_vma=False,
    )
```

```python
import math

import jax
import jax.numpy as jnp
import numpy as np
from jax import lax
from jax.experimental import pallas as pl
from jax.experimental.pallas import tpu as pltpu
from jax.sharding import PartitionSpec as P

MESH = pl.DeviceIdType.MESH
BF = jnp.bfloat16
F32 = jnp.float32

NX = 8
PAIRS = 4
CY = 128
CZ = 256
K = 128
BY = 2
CAP = 4
SLOT = 2 * BY * CAP
NG = 32
NC = 8
UNITS = 16
PARTS = ((0, 1), (1, 3), (3, 4))


def split(value):
    high = value.astype(BF)
    return high, (value - high.astype(F32)).astype(BF)


NN = (((1,), (0,)), ((), ()))
NT = (((1,), (1,)), ((), ()))


def dot(a, b, dims=NN):
    return lax.dot_general(a, b, dims, preferred_element_type=F32)


def dot3(ah, al, bh, bl, dims=NN):
    return dot(ah, bh, dims) + dot(ah, bl, dims) + dot(al, bh, dims)


def cmul(a, b):
    return (a[0] * b[0] - a[1] * b[1], a[0] * b[1] + a[1] * b[0])


def cadd(a, b):
    return (a[0] + b[0], a[1] + b[1])


def cinv(a):
    modulus = a[0] * a[0] + a[1] * a[1]
    return (a[0] / modulus, -a[1] / modulus)


def chain(count, stride, edges):
    shape = (count, 128)
    place = lax.broadcasted_iota(jnp.int32, shape, 0)
    lane = lax.broadcasted_iota(jnp.int32, shape, 1) - stride * place
    one = jnp.ones(shape, F32)
    zero = jnp.zeros(shape, F32)
    head = ((lane == 0).astype(F32), (lane == 1).astype(F32))
    tail = ((lane == 2).astype(F32), (lane == 3).astype(F32))
    lead_left, tail_left, lead_right, tail_right = edges

    def shifted(value, by, fill):
        if by > 0:
            return jnp.where(place >= by, pltpu.roll(value, by, 0), fill)
        return jnp.where(place < count + by, pltpu.roll(value, count + by, 0), fill)

    def moved(value, by, fill):
        return (shifted(value[0], by, fill), shifted(value[1], by, zero))

    a, b = cmul(tail_left, lead_right), cmul(tail_right, lead_left)
    m = [(a[0] - b[0], a[1] - b[1]), tail_right, (-lead_left[0], -lead_left[1]), (one, zero)]
    by = 1
    while by < count:
        q = [moved(m[0], by, one), moved(m[1], by, zero), moved(m[2], by, zero), moved(m[3], by, one)]
        m = [
            cadd(cmul(m[0], q[0]), cmul(m[1], q[2])),
            cadd(cmul(m[0], q[1]), cmul(m[1], q[3])),
            cadd(cmul(m[2], q[0]), cmul(m[3], q[2])),
            cadd(cmul(m[2], q[1]), cmul(m[3], q[3])),
        ]
        by *= 2
    coupling = cmul(moved(m[1], 1, zero), cinv(moved(m[3], 1, one)))

    def affine(factor, addend, sign):
        by = 1
        while by < count:
            before = (moved(factor, sign * by, one), moved(addend, sign * by, zero))
            addend = cadd(cmul(factor, before[1]), addend)
            factor = cmul(factor, before[0])
            by *= 2
        return addend

    step = cmul(lead_left, coupling)
    inverse = cinv((1.0 - step[0], -step[1]))
    gain = cmul(tail_left, inverse)
    carried = moved(affine(gain, cadd(tail, cmul(cmul(gain, coupling), head)), 1), 1, zero)
    offset = cmul(cadd(head, cmul(lead_left, carried)), inverse)
    value = affine(cmul(lead_right, inverse), offset, -1)
    return cadd(carried, cmul(coupling, value)), moved(value, -1, zero)


def embed(target, size, real, imag):
    for n, piece in enumerate(split(real)):
        target[n, 0:size, 0:size] = piece
        target[n, size:, size:] = piece
    for n, piece in enumerate(split(imag)):
        target[n, 0:size, size:] = -piece
        target[n, size:, 0:size] = piece


def embed_edges(target, wide, size, source):
    wide[...] = jnp.zeros_like(wide)
    for n, r in enumerate((0, size - 1)):
        wide[2 * n : 2 * n + 1, 0:size] = source[0, r : r + 1, :]
        wide[2 * n : 2 * n + 1, size:] = -source[1, r : r + 1, :]
        wide[2 * n + 1 : 2 * n + 2, 0:size] = source[1, r : r + 1, :]
        wide[2 * n + 1 : 2 * n + 2, size:] = source[0, r : r + 1, :]
    target[0], target[1] = split(wide[...])


def rows_of(block):
    k = lax.broadcasted_iota(jnp.int32, (1, SLOT * NG), 1)
    row = (k // BY) % 2 * K + k % BY
    row = jnp.where(block > 0.5, row.astype(F32) + BY * (block - 1.0), -1.0)
    place = lax.broadcasted_iota(jnp.int32, (2 * K, SLOT * NG), 0).astype(F32)
    return (place == row).astype(F32)


def kernel(
    links,
    wave_hbm,
    absorber_hbm,
    row_hbm,
    column_hbm,
    blocks_hbm,
    owners_hbm,
    phase_hbm,
    tables_hbm,
    damped_hbm,
    spectrum_hbm,
    wave,
    absorber,
    row,
    column,
    top,
    bottom,
    listed,
    owners,
    phase,
    tables,
    yemb,
    ywide,
    yedge,
    spikes,
    psi,
    heads,
    gathered,
    edge_line,
    edges,
    edge_rows,
    flat_a,
    flat_v,
    values_out,
    values_in,
    solved,
    field,
    zemb,
    zwide,
    zedge,
    zheads,
    zall,
    zcorner,
    zresponse,
    square,
    zspike,
    zfix,
    padded,
    pick,
    damped,
    outgoing,
    incoming,
    ytab,
    volkov,
    spectrum,
    load_sem,
    damped_sem,
    spectrum_sem,
    edge_sem,
    head_sem,
    value_sem,
    z_send,
    z_recv,
    block_send,
    block_recv,
):
    me = lax.axis_index("gy")
    mez = lax.axis_index("gz")
    half = me // UNITS
    base = half * UNITS
    unit = me - base

    barrier = pltpu.get_barrier_semaphore()

    def greet(s, carry):
        pl.semaphore_signal(
            barrier, inc=1, device_id={"gy": lax.rem(me + s, NG)}, device_id_type=MESH
        )
        return carry

    def greet_z(s, carry):
        pl.semaphore_signal(
            barrier, inc=1, device_id={"gz": lax.rem(mez + s, NC)}, device_id_type=MESH
        )
        return carry

    def load(number, source, target):
        copy = pltpu.make_async_copy(source, target, load_sem.at[number])
        copy.start()
        return copy

    row_load = load(0, row_hbm, row)
    wave_loads = [load(9 + x, wave_hbm.at[:, x], wave.at[:, x]) for x in range(NX)]
    lax.fori_loop(1, NG, greet, 0)
    lax.fori_loop(1, NC, greet_z, 0)
    column_load = load(1, column_hbm.at[:, mez], column)
    top_load = load(2, column_hbm.at[:, :, pl.ds(0, 8), :], top)
    bottom_load = load(3, column_hbm.at[:, :, pl.ds(CZ - 8, 8), :], bottom)
    blocks_load = load(4, blocks_hbm, listed)
    owners_load = load(5, owners_hbm, owners)
    absorber_load = load(6, absorber_hbm, absorber)
    tables_load = load(7, tables_hbm, tables)
    phase_load = load(8, phase_hbm, phase)

    row_load.wait()
    embed_edges(yedge, ywide, CY, row)
    lane = lax.broadcasted_iota(jnp.int32, (1, 128), 1)
    edge_row = jnp.zeros((1, 128), F32)
    for side, place in enumerate((0, CY - 1)):
        link = (links[0, side, 0], links[0, side, 1])
        spike = cmul(link, (row[0, :, place : place + 1], row[1, :, place : place + 1]))
        for part in range(2):
            spikes[2 * side + part] = jnp.broadcast_to(spike[part], (CY, 128))
            for n, r in enumerate((0, CY - 1)):
                term = spikes[2 * side + part, r : r + 1, :]
                edge_row = jnp.where(lane == 4 * side + 2 * n + part, term, edge_row)
    edge_line[0] = edge_row

    for x in range(NX):
        wave_loads[x].wait()
        high, low = split(jnp.concatenate([wave[0, x], wave[1, x]], axis=0))
        psi[0, x], psi[1, x] = high, low
        found = dot3(yedge[0], yedge[1], high, low)
        for h in range(2):
            heads[2 * x + h] = found[0:4, 128 * h : 128 * h + 128]

    pl.semaphore_wait(barrier, NG - 1 + NC - 1)

    def send_edges(s, carry):
        pltpu.make_async_remote_copy(
            src_ref=edge_line,
            dst_ref=edges.at[pl.ds(me, 1)],
            send_sem=edge_sem.at[0],
            recv_sem=edge_sem.at[1],
            device_id={"gy": lax.rem(me + s, NG)},
            device_id_type=MESH,
        ).start()
        return carry

    lax.fori_loop(1, NG, send_edges, 0)
    edges[me] = edge_row

    def send_heads(s, carry):
        peer = lax.rem(me + s, NG)
        pltpu.make_async_remote_copy(
            src_ref=heads.at[lax.rem(peer, UNITS)],
            dst_ref=gathered.at[me],
            send_sem=head_sem.at[0],
            recv_sem=head_sem.at[1],
            device_id={"gy": peer},
            device_id_type=MESH,
        ).start()
        return carry

    lax.fori_loop(1, NG, send_heads, 0)
    gathered[me] = heads[unit]

    pltpu.make_async_copy(
        edges.at[pl.ds(0, NG - 1)], edges.at[pl.ds(0, NG - 1)], edge_sem.at[1]
    ).wait()
    for j in range(NG):
        edge_rows[j : j + 1, :] = edges[j]
    wide = [jnp.broadcast_to(edge_rows[:, i : i + 1], (NG, 128)) for i in range(8)]
    left, right = chain(NG, 4, [(wide[i], wide[i + 1]) for i in (0, 2, 4, 6)])
    for i, value in enumerate(left + right):
        flat_a[pl.ds(i, NG, stride=4), :] = value
    embed(yemb, CY, row[0], row[1])
    for x in range(NX):
        solved[x] = dot3(yemb[0], yemb[1], psi[0, x], psi[1, x])

    pltpu.make_async_copy(
        gathered.at[pl.ds(0, NG - 1)], gathered.at[pl.ds(0, NG - 1)], head_sem.at[1]
    ).wait()
    for j in range(NG):
        flat_v[4 * j : 4 * j + 4, :] = gathered[j]
    ah, al = split(flat_a[...])
    vh, vl = split(flat_v[...])
    found = dot3(ah, al, vh, vl)
    for j in range(NG):
        values_out[j] = found[4 * j : 4 * j + 4, :]

    def send_values(s, carry):
        peer = base + lax.rem(unit + s, UNITS)
        pltpu.make_async_remote_copy(
            src_ref=values_out.at[peer],
            dst_ref=values_in.at[unit],
            send_sem=value_sem.at[0],
            recv_sem=value_sem.at[1],
            device_id={"gy": peer},
            device_id_type=MESH,
        ).start()
        return carry

    lax.fori_loop(1, UNITS, send_values, 0)
    values_in[unit] = values_out[me]

    column_load.wait()
    embed(zemb, CZ, column[0], column[1])
    embed_edges(zedge, zwide, CZ, column)
    for side in range(2):
        link = (links[1, side, 0], links[1, side, 1])
        lines = []
        for part in range(2):
            pieces = []
            for a in range(2):
                turned = jnp.transpose(
                    column[part, 128 * a : 128 * a + 128, 128 * side : 128 * side + 128]
                )
                pieces.append(turned[0:1, :] if side == 0 else turned[127:128, :])
            lines.append(jnp.concatenate(pieces, axis=1))
        spike = cmul(link, (lines[0], lines[1]))
        zspike[2 * side : 2 * side + 1, 0:CZ] = spike[0]
        zspike[2 * side : 2 * side + 1, CZ:] = spike[1]
        zspike[2 * side + 1 : 2 * side + 2, 0:CZ] = -spike[1]
        zspike[2 * side + 1 : 2 * side + 2, CZ:] = spike[0]

    top_load.wait()
    bottom_load.wait()
    terms = []
    for side, place in enumerate((0, CZ - 1)):
        link = (links[1, side, 0], links[1, side, 1])
        for table, r in ((top, 0), (bottom, 7)):
            for part in range(2):
                for c in range(NC):
                    lanes = 128 * side
                    zcorner[part, c : c + 1, :] = table[part, c, r : r + 1, lanes : lanes + 128]
            at = place % 128
            value = tuple(
                jnp.broadcast_to(zcorner[part][:, at : at + 1], (NC, 128)) for part in range(2)
            )
            terms.append(cmul(link, value))
    left, right = chain(NC, 8, terms)
    square[...] = jnp.zeros_like(square)
    for i, value in enumerate(left + right):
        zresponse[i] = value
        square[i : i + 1, :] = zresponse[i, pl.ds(mez, 1), :]
    turned = jnp.transpose(square[...])
    held = jnp.zeros((64, 2 * CZ), F32)
    for i in range(4):
        held = held + turned[0:64, i : i + 1] * zspike[i : i + 1, :]
    for h in range(2):
        high, low = split(held if h == 0 else pltpu.roll(held, 4, 0))
        zfix[h, 0:64, :] = high
        zfix[h, 64:128, :] = high
        zfix[h, 128:192, :] = low
        zfix[h, 192:256, :] = low

    blocks_load.wait()
    owners_load.wait()
    padded[...] = jnp.full_like(padded, -1.0)
    count = listed.shape[1]
    padded[0, :, 0:count] = listed[...].astype(F32)
    padded[1, :, 0:count] = owners[...].astype(F32)
    ids, names = (
        jnp.transpose(jnp.broadcast_to(padded[n, pl.ds(me, 1), :], (128, 128))) for n in range(2)
    )
    across = lax.broadcasted_iota(jnp.int32, (128, 128), 1)
    down = lax.broadcasted_iota(jnp.int32, (128, 128), 0)
    same = (names == padded[1, pl.ds(me, 1), :]) & (across < down)
    rank = jnp.sum(same.astype(F32), axis=1, keepdims=True)
    slot = jnp.where(names[:, 0:1] < 0.0, -1.0, CAP * names[:, 0:1] + rank)
    k = lax.broadcasted_iota(jnp.int32, (1, SLOT * NG), 1)
    hit = slot == (k // (2 * BY)).astype(F32)
    block = jnp.sum(jnp.where(hit, ids[:, 0:1] + 1.0, 0.0), axis=0, keepdims=True)
    onehot = rows_of(block)
    for n in range(SLOT * NG // 128):
        for m in range(2):
            pick[128 * n : 128 * n + 128, 128 * m : 128 * m + 128] = jnp.transpose(
                onehot[128 * m : 128 * m + 128, 128 * n : 128 * n + 128]
            ).astype(BF)

    pltpu.make_async_copy(
        values_in.at[pl.ds(0, UNITS - 1)], values_in.at[pl.ds(0, UNITS - 1)], value_sem.at[1]
    ).wait()

    def meet_z(part):
        first, last = PARTS[part]
        for p in range(first, last):
            for x in (2 * p, 2 * p + 1):
                for h in range(2):
                    v = values_in[2 * x + h]
                    lre, lim, rre, rim = (v[i : i + 1, :] for i in range(4))
                    re = solved[x, 0:CY, 128 * h : 128 * h + 128]
                    im = solved[x, CY:, 128 * h : 128 * h + 128]
                    re = re + (spikes[0] * lre - spikes[1] * lim)
                    re = re + (spikes[2] * rre - spikes[3] * rim)
                    im = im + (spikes[0] * lim + spikes[1] * lre)
                    im = im + (spikes[2] * rim + spikes[3] * rre)
                    for c, value in enumerate((re, im)):
                        high, low = split(value)
                        at = CZ * c + 128 * h
                        field[0, x, :, at : at + 128] = high
                        field[1, x, :, at : at + 128] = low
                found = dot3(zedge[0], zedge[1], field[0, x], field[1, x], NT)
                zheads[p, 4 * (x % 2) : 4 * (x % 2) + 4, :] = found[0:4, :]

        def send_zheads(s, carry):
            pltpu.make_async_remote_copy(
                src_ref=zheads.at[pl.ds(first, last - first)],
                dst_ref=zall.at[mez, pl.ds(first, last - first)],
                send_sem=z_send.at[part],
                recv_sem=z_recv.at[part],
                device_id={"gz": lax.rem(mez + s, NC)},
                device_id_type=MESH,
            ).start()
            return carry

        lax.fori_loop(1, NC, send_zheads, 0)
        for p in range(first, last):
            zall[mez, p] = zheads[p]

    stores = []
    meet_z(0)
    for part, (first, last) in enumerate(PARTS):
        if part + 1 < len(PARTS):
            meet_z(part + 1)
        planes = pl.ds(2 * first, 2 * (last - first))
        for x in range(2 * first, 2 * last):
            solved[x, 0:CY, :] = dot3(
                field[0, x], field[1, x], zemb[0, 0:CZ, :], zemb[1, 0:CZ, :], NT
            )
            solved[x, CY:, :] = dot3(
                field[0, x], field[1, x], zemb[0, CZ:, :], zemb[1, CZ:, :], NT
            )
        if part == 0:
            absorber_load.wait()
        view = zall.at[pl.ds(0, NC - 1), pl.ds(first, last - first)]
        pltpu.make_async_copy(view, view, z_recv.at[part]).wait()
        for p in range(first, last):
            g = zall[:, p].reshape(8 * NC, 128)
            high = g.astype(BF).astype(F32)
            turned = jnp.transpose(jnp.concatenate([high, g - high], axis=0)).astype(BF)
            turned = jnp.concatenate([turned, turned], axis=1)
            folded = []
            for x in (2 * p, 2 * p + 1):
                fix = dot(turned, zfix[x % 2])
                kept = jnp.exp(-absorber[x])
                rows = []
                for c in range(2):
                    value = solved[x, CY * c : CY * c + CY, :] + fix[:, CZ * c : CZ * c + CZ]
                    left = value * kept
                    damped[c, x] = left
                    lost = value - left
                    rows.append(lost[:, 0:128] + lost[:, 128:256])
                folded.append(jnp.concatenate(rows, axis=0))
            high, low = split(jnp.concatenate(folded, axis=1))
            chosen = dot(pick[...], high) + dot(pick[...], low)
            for n in range(2):
                outgoing[2 * p + n] = chosen[:, 128 * n : 128 * n + 128].reshape(NG, SLOT, 128)

        def send_blocks(s, carry):
            peer = lax.rem(me + s, NG)
            pltpu.make_async_remote_copy(
                src_ref=outgoing.at[planes, peer],
                dst_ref=incoming.at[planes, me],
                send_sem=block_send.at[part],
                recv_sem=block_recv.at[part],
                device_id={"gy": peer},
                device_id_type=MESH,
            ).start()
            return carry

        lax.fori_loop(1, NG, send_blocks, 0)
        for x in range(2 * first, 2 * last):
            incoming[x, me] = outgoing[x, me]
        store = pltpu.make_async_copy(
            damped.at[:, planes], damped_hbm.at[:, planes], damped_sem.at[part]
        )
        store.start()
        stores.append(store)

    source = lax.broadcasted_iota(jnp.int32, (NG, SLOT * NG), 0)
    mine = (padded[1] == me.astype(F32)).astype(F32)
    rank = dot(mine.astype(BF), (down < across).astype(F32).astype(BF))
    total = jnp.zeros((NG, SLOT * NG), F32)
    for n in range(CAP):
        hit = jnp.where(rank == float(n), mine, 0.0)
        found = jnp.sum(hit * (padded[0] + 1.0), axis=1, keepdims=True)
        total = total + jnp.where((k // (2 * BY)) % CAP == n, found, 0.0)
    total = jnp.where(k // SLOT == source, total, 0.0)
    onehot = rows_of(jnp.sum(total, axis=0, keepdims=True)).astype(BF)
    tables_load.wait()
    for n in range(2):
        ytab[n] = dot(tables[n], onehot).astype(BF)
    phase_load.wait()
    norm = 1.0 / math.sqrt(CY * CZ)
    volkov[0] = jnp.cos(phase[...])
    volkov[1] = jnp.sin(phase[...])

    for part, (first, last) in enumerate(PARTS):
        planes = pl.ds(2 * first, 2 * (last - first))
        view = incoming.at[planes, pl.ds(0, NG - 1)]
        pltpu.make_async_copy(view, view, block_recv.at[part]).wait()
        for p in range(first, last):
            both = [incoming[2 * p + n].reshape(SLOT * NG, 128) for n in range(2)]
            high, low = split(jnp.concatenate(both, axis=1))
            along_y = dot3(ytab[0], ytab[1], high, low)
            lines = [
                jnp.concatenate(
                    [along_y[0:K, 128 * n : 128 * n + 128], along_y[K:, 128 * n : 128 * n + 128]],
                    axis=1,
                )
                for n in range(2)
            ]
            high, low = split(jnp.concatenate(lines, axis=0))
            both = dot3(high, low, tables[2], tables[3])
            for n in range(2):
                value = (both[K * n : K * n + K, 0:K], both[K * n : K * n + K, K:])
                re, im = cmul((volkov[0], volkov[1]), value)
                spectrum[0, 2 * p + n] = re * norm
                spectrum[1, 2 * p + n] = im * norm
        store = pltpu.make_async_copy(
            spectrum.at[:, planes], spectrum_hbm.at[:, planes], spectrum_sem.at[part]
        )
        store.start()
        stores.append(store)

    def sent(view, sem):
        pltpu.make_async_copy(view, view, sem).wait()

    sent(edges.at[pl.ds(0, NG - 1)], edge_sem.at[0])
    sent(gathered.at[pl.ds(0, NG - 1)], head_sem.at[0])
    sent(values_in.at[pl.ds(0, UNITS - 1)], value_sem.at[0])
    for part, (first, last) in enumerate(PARTS):
        sent(zall.at[pl.ds(0, NC - 1), pl.ds(first, last - first)], z_send.at[part])
        planes = pl.ds(2 * first, 2 * (last - first))
        sent(outgoing.at[planes, pl.ds(0, NG - 1)], block_send.at[part])
    for store in stores:
        store.wait()


def phase_tables():
    n, k = np.arange(K)[:, None], np.arange(K)[None, :]
    angle = 2.0 * np.pi / K * ((n * k) % K) - np.pi * (n % 2)
    re, im = np.cos(angle), -np.sin(angle)
    along_y = np.block([[re.T, -im.T], [im.T, re.T]]).astype(np.float32)
    along_z = np.block([[re, im], [-im, re]]).astype(np.float32)
    found = []
    for table in (along_y, along_z):
        high = table.astype(BF)
        found += [high, (table - high.astype(np.float32)).astype(BF)]
    return np.stack(found)


def body(
    wavefunction,
    absorber,
    row_inverse,
    column_inverse,
    link_terms,
    shell_blocks,
    owner_map,
    volkov_phase,
):
    count = shell_blocks.shape[2]
    any_space = pl.BlockSpec(memory_space=pl.ANY)
    smem = pl.BlockSpec(memory_space=pltpu.SMEM)
    V = pltpu.VMEM
    dma = pltpu.SemaphoreType.DMA
    parts = len(PARTS)
    return pl.pallas_call(
        kernel,
        out_shape=(
            jax.ShapeDtypeStruct((2, NX, CY, CZ), F32),
            jax.ShapeDtypeStruct((2, NX, K, K), F32),
        ),
        in_specs=[smem] + [pl.BlockSpec(memory_space=pltpu.HBM)] * 8,
        out_specs=(any_space, any_space),
        scratch_shapes=[
            V((2, NX, CY, CZ), F32),
            V((NX, CY, CZ), F32),
            V((2, CY, CY), F32),
            V((2, CZ, CZ), F32),
            V((2, NC, 8, CZ), F32),
            V((2, NC, 8, CZ), F32),
            V((NG, count), jnp.int32),
            V((NG, count), jnp.int32),
            V((K, K), F32),
            V((4, 2 * K, 2 * K), BF),
            V((2, 2 * CY, 2 * CY), BF),
            V((16, 2 * CY), F32),
            V((2, 16, 2 * CY), BF),
            V((4, CY, 128), F32),
            V((2, NX, 2 * CY, CZ), BF),
            V((UNITS, 4, 128), F32),
            V((NG, 4, 128), F32),
            V((1, 1, 128), F32),
            V((NG, 1, 128), F32),
            V((NG, 128), F32),
            V((4 * NG, 128), F32),
            V((4 * NG, 128), F32),
            V((NG, 4, 128), F32),
            V((UNITS, 4, 128), F32),
            V((NX, 2 * CY, CZ), F32),
            V((2, NX, CY, 2 * CZ), BF),
            V((2, 2 * CZ, 2 * CZ), BF),
            V((16, 2 * CZ), F32),
            V((2, 16, 2 * CZ), BF),
            V((PAIRS, 8, 128), F32),
            V((NC, PAIRS, 8, 128), F32),
            V((2, NC, 128), F32),
            V((4, NC, 128), F32),
            V((128, 128), F32),
            V((4, 2 * CZ), F32),
            V((2, 256, 2 * CZ), BF),
            V((2, NG, 128), F32),
            V((SLOT * NG, 2 * K), BF),
            V((2, NX, CY, CZ), F32),
            V((NX, NG, SLOT, 128), F32),
            V((NX, NG, SLOT, 128), F32),
            V((2, 2 * K, SLOT * NG), BF),
            V((2, K, K), F32),
            V((2, NX, K, K), F32),
            dma((9 + NX,)),
            dma((parts,)),
            dma((parts,)),
            dma((2,)),
            dma((2,)),
            dma((2,)),
            dma((parts,)),
            dma((parts,)),
            dma((parts,)),
            dma((parts,)),
        ],
        compiler_params=pltpu.CompilerParams(
            collective_id=0, has_side_effects=True, vmem_limit_bytes=60 * 1024 * 1024
        ),
    )(
        link_terms,
        wavefunction,
        absorber,
        row_inverse,
        column_inverse.reshape(2, NC, CZ, CZ),
        shell_blocks.reshape(NG, count),
        owner_map.reshape(NG, count),
        volkov_phase,
        phase_tables(),
    )


def solution(mesh):
    placed = (
        P(None, None, "gy", "gz"),
        P(None, "gy", "gz"),
        P(None, "gy", None),
        P(),
        P(),
        P("gz", None, None),
        P("gz", None, None, None),
        P(),
    )
    return jax.shard_map(
        body,
        mesh=mesh,
        in_specs=placed,
        out_specs=(P(None, None, "gy", "gz"), P(None, "gy", "gz", None)),
        check_vma=False,
    )
```

```python
import math

import jax
import jax.numpy as jnp
import numpy as np
from jax import lax
from jax.experimental import pallas as pl
from jax.experimental.pallas import tpu as pltpu
from jax.sharding import PartitionSpec as P

MESH = pl.DeviceIdType.MESH
BF = jnp.bfloat16
F32 = jnp.float32

NX = 8
PAIRS = 4
CY = 128
CZ = 256
K = 128
BY = 2
CAP = 4
SLOT = 2 * BY * CAP
NG = 32
NC = 8
UNITS = 16
PARTS = ((0, 1), (1, 3), (3, 4))


def split(value):
    high = value.astype(BF)
    return high, (value - high.astype(F32)).astype(BF)


NN = (((1,), (0,)), ((), ()))
NT = (((1,), (1,)), ((), ()))


def dot(a, b, dims=NN):
    return lax.dot_general(a, b, dims, preferred_element_type=F32)


def dot3(ah, al, bh, bl, dims=NN):
    return dot(ah, bh, dims) + dot(ah, bl, dims) + dot(al, bh, dims)


def cmul(a, b):
    return (a[0] * b[0] - a[1] * b[1], a[0] * b[1] + a[1] * b[0])


def cadd(a, b):
    return (a[0] + b[0], a[1] + b[1])


def cinv(a):
    modulus = a[0] * a[0] + a[1] * a[1]
    return (a[0] / modulus, -a[1] / modulus)


def chain(count, stride, edges):
    shape = (count, 128)
    place = lax.broadcasted_iota(jnp.int32, shape, 0)
    lane = lax.broadcasted_iota(jnp.int32, shape, 1) - stride * place
    one = jnp.ones(shape, F32)
    zero = jnp.zeros(shape, F32)
    head = ((lane == 0).astype(F32), (lane == 1).astype(F32))
    tail = ((lane == 2).astype(F32), (lane == 3).astype(F32))
    lead_left, tail_left, lead_right, tail_right = edges

    def shifted(value, by, fill):
        if by > 0:
            return jnp.where(place >= by, pltpu.roll(value, by, 0), fill)
        return jnp.where(place < count + by, pltpu.roll(value, count + by, 0), fill)

    def moved(value, by, fill):
        return (shifted(value[0], by, fill), shifted(value[1], by, zero))

    a, b = cmul(tail_left, lead_right), cmul(tail_right, lead_left)
    m = [(a[0] - b[0], a[1] - b[1]), tail_right, (-lead_left[0], -lead_left[1]), (one, zero)]
    by = 1
    while by < count:
        q = [moved(m[0], by, one), moved(m[1], by, zero), moved(m[2], by, zero), moved(m[3], by, one)]
        m = [
            cadd(cmul(m[0], q[0]), cmul(m[1], q[2])),
            cadd(cmul(m[0], q[1]), cmul(m[1], q[3])),
            cadd(cmul(m[2], q[0]), cmul(m[3], q[2])),
            cadd(cmul(m[2], q[1]), cmul(m[3], q[3])),
        ]
        by *= 2
    coupling = cmul(moved(m[1], 1, zero), cinv(moved(m[3], 1, one)))

    def affine(factor, addend, sign):
        by = 1
        while by < count:
            before = (moved(factor, sign * by, one), moved(addend, sign * by, zero))
            addend = cadd(cmul(factor, before[1]), addend)
            factor = cmul(factor, before[0])
            by *= 2
        return addend

    step = cmul(lead_left, coupling)
    inverse = cinv((1.0 - step[0], -step[1]))
    gain = cmul(tail_left, inverse)
    carried = moved(affine(gain, cadd(tail, cmul(cmul(gain, coupling), head)), 1), 1, zero)
    offset = cmul(cadd(head, cmul(lead_left, carried)), inverse)
    value = affine(cmul(lead_right, inverse), offset, -1)
    return cadd(carried, cmul(coupling, value)), moved(value, -1, zero)


def embed(target, size, real, imag):
    for n, piece in enumerate(split(real)):
        target[n, 0:size, 0:size] = piece
        target[n, size:, size:] = piece
    for n, piece in enumerate(split(imag)):
        target[n, 0:size, size:] = -piece
        target[n, size:, 0:size] = piece


def embed_edges(target, wide, size, source):
    wide[...] = jnp.zeros_like(wide)
    for n, r in enumerate((0, size - 1)):
        wide[2 * n : 2 * n + 1, 0:size] = source[0, r : r + 1, :]
        wide[2 * n : 2 * n + 1, size:] = -source[1, r : r + 1, :]
        wide[2 * n + 1 : 2 * n + 2, 0:size] = source[1, r : r + 1, :]
        wide[2 * n + 1 : 2 * n + 2, size:] = source[0, r : r + 1, :]
    target[0], target[1] = split(wide[...])


def rows_of(block):
    k = lax.broadcasted_iota(jnp.int32, (1, SLOT * NG), 1)
    row = (k // BY) % 2 * K + k % BY
    row = jnp.where(block > 0.5, row.astype(F32) + BY * (block - 1.0), -1.0)
    place = lax.broadcasted_iota(jnp.int32, (2 * K, SLOT * NG), 0).astype(F32)
    return (place == row).astype(F32)


def kernel(
    links,
    wave_hbm,
    absorber_hbm,
    row_hbm,
    column_hbm,
    blocks_hbm,
    owners_hbm,
    phase_hbm,
    tables_hbm,
    damped_hbm,
    spectrum_hbm,
    wave,
    absorber,
    row,
    column,
    top,
    bottom,
    listed,
    owners,
    phase,
    tables,
    yemb,
    ywide,
    yedge,
    spikes,
    psi,
    heads,
    gathered,
    edge_line,
    edges,
    edge_rows,
    flat_a,
    flat_v,
    values_out,
    values_in,
    solved,
    field,
    zemb,
    zwide,
    zedge,
    zheads,
    zall,
    zcorner,
    zresponse,
    square,
    zspike,
    zfix,
    padded,
    pick,
    damped,
    outgoing,
    incoming,
    ytab,
    volkov,
    spectrum,
    load_sem,
    damped_sem,
    spectrum_sem,
    edge_sem,
    head_sem,
    value_sem,
    z_send,
    z_recv,
    block_send,
    block_recv,
):
    me = lax.axis_index("gy")
    mez = lax.axis_index("gz")
    half = me // UNITS
    base = half * UNITS
    unit = me - base

    barrier = pltpu.get_barrier_semaphore()

    def greet(s, carry):
        pl.semaphore_signal(
            barrier, inc=1, device_id={"gy": lax.rem(me + s, NG)}, device_id_type=MESH
        )
        return carry

    def greet_z(s, carry):
        pl.semaphore_signal(
            barrier, inc=1, device_id={"gz": lax.rem(mez + s, NC)}, device_id_type=MESH
        )
        return carry

    def load(number, source, target):
        copy = pltpu.make_async_copy(source, target, load_sem.at[number])
        copy.start()
        return copy

    row_load = load(0, row_hbm, row)
    wave_loads = [load(9 + x, wave_hbm.at[:, x], wave.at[:, x]) for x in range(NX)]
    lax.fori_loop(1, NG, greet, 0)
    lax.fori_loop(1, NC, greet_z, 0)
    column_load = load(1, column_hbm.at[:, mez], column)
    top_load = load(2, column_hbm.at[:, :, pl.ds(0, 8), :], top)
    bottom_load = load(3, column_hbm.at[:, :, pl.ds(CZ - 8, 8), :], bottom)
    blocks_load = load(4, blocks_hbm, listed)
    owners_load = load(5, owners_hbm, owners)
    absorber_load = load(6, absorber_hbm, absorber)
    tables_load = load(7, tables_hbm, tables)
    phase_load = load(8, phase_hbm, phase)

    row_load.wait()
    embed_edges(yedge, ywide, CY, row)
    lane = lax.broadcasted_iota(jnp.int32, (1, 128), 1)
    edge_row = jnp.zeros((1, 128), F32)
    for side, place in enumerate((0, CY - 1)):
        link = (links[0, side, 0], links[0, side, 1])
        spike = cmul(link, (row[0, :, place : place + 1], row[1, :, place : place + 1]))
        for part in range(2):
            spikes[2 * side + part] = jnp.broadcast_to(spike[part], (CY, 128))
            for n, r in enumerate((0, CY - 1)):
                term = spikes[2 * side + part, r : r + 1, :]
                edge_row = jnp.where(lane == 4 * side + 2 * n + part, term, edge_row)
    edge_line[0] = edge_row

    for x in range(NX):
        wave_loads[x].wait()
        high, low = split(jnp.concatenate([wave[0, x], wave[1, x]], axis=0))
        psi[0, x], psi[1, x] = high, low
        found = dot3(yedge[0], yedge[1], high, low)
        for h in range(2):
            heads[2 * x + h] = found[0:4, 128 * h : 128 * h + 128]

    pl.semaphore_wait(barrier, NG - 1 + NC - 1)

    def send_edges(s, carry):
        pltpu.make_async_remote_copy(
            src_ref=edge_line,
            dst_ref=edges.at[pl.ds(me, 1)],
            send_sem=edge_sem.at[0],
            recv_sem=edge_sem.at[1],
            device_id={"gy": lax.rem(me + s, NG)},
            device_id_type=MESH,
        ).start()
        return carry

    lax.fori_loop(1, NG, send_edges, 0)
    edges[me] = edge_row

    def send_heads(s, carry):
        peer = lax.rem(me + s, NG)
        pltpu.make_async_remote_copy(
            src_ref=heads.at[lax.rem(peer, UNITS)],
            dst_ref=gathered.at[me],
            send_sem=head_sem.at[0],
            recv_sem=head_sem.at[1],
            device_id={"gy": peer},
            device_id_type=MESH,
        ).start()
        return carry

    lax.fori_loop(1, NG, send_heads, 0)
    gathered[me] = heads[unit]

    pltpu.make_async_copy(
        edges.at[pl.ds(0, NG - 1)], edges.at[pl.ds(0, NG - 1)], edge_sem.at[1]
    ).wait()
    for j in range(NG):
        edge_rows[j : j + 1, :] = edges[j]
    wide = [jnp.broadcast_to(edge_rows[:, i : i + 1], (NG, 128)) for i in range(8)]
    left, right = chain(NG, 4, [(wide[i], wide[i + 1]) for i in (0, 2, 4, 6)])
    for i, value in enumerate(left + right):
        flat_a[pl.ds(i, NG, stride=4), :] = value
    embed(yemb, CY, row[0], row[1])
    for x in range(NX):
        solved[x] = dot3(yemb[0], yemb[1], psi[0, x], psi[1, x])

    pltpu.make_async_copy(
        gathered.at[pl.ds(0, NG - 1)], gathered.at[pl.ds(0, NG - 1)], head_sem.at[1]
    ).wait()
    for j in range(NG):
        flat_v[4 * j : 4 * j + 4, :] = gathered[j]
    ah, al = split(flat_a[...])
    vh, vl = split(flat_v[...])
    found = dot3(ah, al, vh, vl)
    for j in range(NG):
        values_out[j] = found[4 * j : 4 * j + 4, :]

    def send_values(s, carry):
        peer = base + lax.rem(unit + s, UNITS)
        pltpu.make_async_remote_copy(
            src_ref=values_out.at[peer],
            dst_ref=values_in.at[unit],
            send_sem=value_sem.at[0],
            recv_sem=value_sem.at[1],
            device_id={"gy": peer},
            device_id_type=MESH,
        ).start()
        return carry

    lax.fori_loop(1, UNITS, send_values, 0)
    values_in[unit] = values_out[me]

    column_load.wait()
    embed(zemb, CZ, column[0], column[1])
    embed_edges(zedge, zwide, CZ, column)
    for side in range(2):
        link = (links[1, side, 0], links[1, side, 1])
        lines = []
        for part in range(2):
            pieces = []
            for a in range(2):
                turned = jnp.transpose(
                    column[part, 128 * a : 128 * a + 128, 128 * side : 128 * side + 128]
                )
                pieces.append(turned[0:1, :] if side == 0 else turned[127:128, :])
            lines.append(jnp.concatenate(pieces, axis=1))
        spike = cmul(link, (lines[0], lines[1]))
        zspike[2 * side : 2 * side + 1, 0:CZ] = spike[0]
        zspike[2 * side : 2 * side + 1, CZ:] = spike[1]
        zspike[2 * side + 1 : 2 * side + 2, 0:CZ] = -spike[1]
        zspike[2 * side + 1 : 2 * side + 2, CZ:] = spike[0]

    top_load.wait()
    bottom_load.wait()
    terms = []
    for side, place in enumerate((0, CZ - 1)):
        link = (links[1, side, 0], links[1, side, 1])
        for table, r in ((top, 0), (bottom, 7)):
            for part in range(2):
                for c in range(NC):
                    lanes = 128 * side
                    zcorner[part, c : c + 1, :] = table[part, c, r : r + 1, lanes : lanes + 128]
            at = place % 128
            value = tuple(
                jnp.broadcast_to(zcorner[part][:, at : at + 1], (NC, 128)) for part in range(2)
            )
            terms.append(cmul(link, value))
    left, right = chain(NC, 8, terms)
    square[...] = jnp.zeros_like(square)
    for i, value in enumerate(left + right):
        zresponse[i] = value
        square[i : i + 1, :] = zresponse[i, pl.ds(mez, 1), :]
    turned = jnp.transpose(square[...])
    held = jnp.zeros((64, 2 * CZ), F32)
    for i in range(4):
        held = held + turned[0:64, i : i + 1] * zspike[i : i + 1, :]
    for h in range(2):
        high, low = split(held if h == 0 else pltpu.roll(held, 4, 0))
        zfix[h, 0:64, :] = high
        zfix[h, 64:128, :] = high
        zfix[h, 128:192, :] = low
        zfix[h, 192:256, :] = low

    blocks_load.wait()
    owners_load.wait()
    padded[...] = jnp.full_like(padded, -1.0)
    count = listed.shape[1]
    padded[0, :, 0:count] = listed[...].astype(F32)
    padded[1, :, 0:count] = owners[...].astype(F32)
    ids, names = (
        jnp.transpose(jnp.broadcast_to(padded[n, pl.ds(me, 1), :], (128, 128))) for n in range(2)
    )
    across = lax.broadcasted_iota(jnp.int32, (128, 128), 1)
    down = lax.broadcasted_iota(jnp.int32, (128, 128), 0)
    same = (names == padded[1, pl.ds(me, 1), :]) & (across < down)
    rank = jnp.sum(same.astype(F32), axis=1, keepdims=True)
    slot = jnp.where(names[:, 0:1] < 0.0, -1.0, CAP * names[:, 0:1] + rank)
    k = lax.broadcasted_iota(jnp.int32, (1, SLOT * NG), 1)
    hit = slot == (k // (2 * BY)).astype(F32)
    block = jnp.sum(jnp.where(hit, ids[:, 0:1] + 1.0, 0.0), axis=0, keepdims=True)
    onehot = rows_of(block)
    for n in range(SLOT * NG // 128):
        for m in range(2):
            pick[128 * n : 128 * n + 128, 128 * m : 128 * m + 128] = jnp.transpose(
                onehot[128 * m : 128 * m + 128, 128 * n : 128 * n + 128]
            ).astype(BF)

    pltpu.make_async_copy(
        values_in.at[pl.ds(0, UNITS - 1)], values_in.at[pl.ds(0, UNITS - 1)], value_sem.at[1]
    ).wait()

    def meet_z(part):
        first, last = PARTS[part]
        for p in range(first, last):
            for x in (2 * p, 2 * p + 1):
                for h in range(2):
                    v = values_in[2 * x + h]
                    lre, lim, rre, rim = (v[i : i + 1, :] for i in range(4))
                    re = solved[x, 0:CY, 128 * h : 128 * h + 128]
                    im = solved[x, CY:, 128 * h : 128 * h + 128]
                    re = re + (spikes[0] * lre - spikes[1] * lim)
                    re = re + (spikes[2] * rre - spikes[3] * rim)
                    im = im + (spikes[0] * lim + spikes[1] * lre)
                    im = im + (spikes[2] * rim + spikes[3] * rre)
                    for c, value in enumerate((re, im)):
                        high, low = split(value)
                        at = CZ * c + 128 * h
                        field[0, x, :, at : at + 128] = high
                        field[1, x, :, at : at + 128] = low
                found = dot3(zedge[0], zedge[1], field[0, x], field[1, x], NT)
                zheads[p, 4 * (x % 2) : 4 * (x % 2) + 4, :] = found[0:4, :]

        def send_zheads(s, carry):
            pltpu.make_async_remote_copy(
                src_ref=zheads.at[pl.ds(first, last - first)],
                dst_ref=zall.at[mez, pl.ds(first, last - first)],
                send_sem=z_send.at[part],
                recv_sem=z_recv.at[part],
                device_id={"gz": lax.rem(mez + s, NC)},
                device_id_type=MESH,
            ).start()
            return carry

        lax.fori_loop(1, NC, send_zheads, 0)
        for p in range(first, last):
            zall[mez, p] = zheads[p]

    stores = []
    meet_z(0)
    for part, (first, last) in enumerate(PARTS):
        if part + 1 < len(PARTS):
            meet_z(part + 1)
        planes = pl.ds(2 * first, 2 * (last - first))
        for x in range(2 * first, 2 * last):
            solved[x, 0:CY, :] = dot3(
                field[0, x], field[1, x], zemb[0, 0:CZ, :], zemb[1, 0:CZ, :], NT
            )
            solved[x, CY:, :] = dot3(
                field[0, x], field[1, x], zemb[0, CZ:, :], zemb[1, CZ:, :], NT
            )
        if part == 0:
            absorber_load.wait()
        view = zall.at[pl.ds(0, NC - 1), pl.ds(first, last - first)]
        pltpu.make_async_copy(view, view, z_recv.at[part]).wait()
        for p in range(first, last):
            g = zall[:, p].reshape(8 * NC, 128)
            high = g.astype(BF).astype(F32)
            turned = jnp.transpose(jnp.concatenate([high, g - high], axis=0)).astype(BF)
            turned = jnp.concatenate([turned, turned], axis=1)
            folded = []
            for x in (2 * p, 2 * p + 1):
                fix = dot(turned, zfix[x % 2])
                kept = jnp.exp(-absorber[x])
                rows = []
                for c in range(2):
                    value = solved[x, CY * c : CY * c + CY, :] + fix[:, CZ * c : CZ * c + CZ]
                    left = value * kept
                    damped[c, x] = left
                    lost = value - left
                    rows.append(lost[:, 0:128] + lost[:, 128:256])
                folded.append(jnp.concatenate(rows, axis=0))
            high, low = split(jnp.concatenate(folded, axis=1))
            chosen = dot(pick[...], high) + dot(pick[...], low)
            for n in range(2):
                outgoing[2 * p + n] = chosen[:, 128 * n : 128 * n + 128].reshape(NG, SLOT, 128)

        def send_blocks(s, carry):
            peer = lax.rem(me + s, NG)
            pltpu.make_async_remote_copy(
                src_ref=outgoing.at[planes, peer],
                dst_ref=incoming.at[planes, me],
                send_sem=block_send.at[part],
                recv_sem=block_recv.at[part],
                device_id={"gy": peer},
                device_id_type=MESH,
            ).start()
            return carry

        lax.fori_loop(1, NG, send_blocks, 0)
        for x in range(2 * first, 2 * last):
            incoming[x, me] = outgoing[x, me]
        store = pltpu.make_async_copy(
            damped.at[:, planes], damped_hbm.at[:, planes], damped_sem.at[part]
        )
        store.start()
        stores.append(store)

    source = lax.broadcasted_iota(jnp.int32, (NG, SLOT * NG), 0)
    mine = (padded[1] == me.astype(F32)).astype(F32)
    rank = dot(mine.astype(BF), (down < across).astype(F32).astype(BF))
    total = jnp.zeros((NG, SLOT * NG), F32)
    for n in range(CAP):
        hit = jnp.where(rank == float(n), mine, 0.0)
        found = jnp.sum(hit * (padded[0] + 1.0), axis=1, keepdims=True)
        total = total + jnp.where((k // (2 * BY)) % CAP == n, found, 0.0)
    total = jnp.where(k // SLOT == source, total, 0.0)
    onehot = rows_of(jnp.sum(total, axis=0, keepdims=True)).astype(BF)
    tables_load.wait()
    for n in range(2):
        ytab[n] = dot(tables[n], onehot).astype(BF)
    phase_load.wait()
    norm = 1.0 / math.sqrt(CY * CZ)
    volkov[0] = jnp.cos(phase[...])
    volkov[1] = jnp.sin(phase[...])

    for part, (first, last) in enumerate(PARTS):
        planes = pl.ds(2 * first, 2 * (last - first))
        view = incoming.at[planes, pl.ds(0, NG - 1)]
        pltpu.make_async_copy(view, view, block_recv.at[part]).wait()
        for p in range(first, last):
            both = [incoming[2 * p + n].reshape(SLOT * NG, 128) for n in range(2)]
            high, low = split(jnp.concatenate(both, axis=1))
            along_y = dot3(ytab[0], ytab[1], high, low)
            lines = [
                jnp.concatenate(
                    [along_y[0:K, 128 * n : 128 * n + 128], along_y[K:, 128 * n : 128 * n + 128]],
                    axis=1,
                )
                for n in range(2)
            ]
            high, low = split(jnp.concatenate(lines, axis=0))
            both = dot3(high, low, tables[2], tables[3])
            for n in range(2):
                value = (both[K * n : K * n + K, 0:K], both[K * n : K * n + K, K:])
                re, im = cmul((volkov[0], volkov[1]), value)
                spectrum[0, 2 * p + n] = re * norm
                spectrum[1, 2 * p + n] = im * norm
        store = pltpu.make_async_copy(
            spectrum.at[:, planes], spectrum_hbm.at[:, planes], spectrum_sem.at[part]
        )
        store.start()
        stores.append(store)

    def sent(view, sem):
        pltpu.make_async_copy(view, view, sem).wait()

    sent(edges.at[pl.ds(0, NG - 1)], edge_sem.at[0])
    sent(gathered.at[pl.ds(0, NG - 1)], head_sem.at[0])
    sent(values_in.at[pl.ds(0, UNITS - 1)], value_sem.at[0])
    for part, (first, last) in enumerate(PARTS):
        sent(zall.at[pl.ds(0, NC - 1), pl.ds(first, last - first)], z_send.at[part])
        planes = pl.ds(2 * first, 2 * (last - first))
        sent(outgoing.at[planes, pl.ds(0, NG - 1)], block_send.at[part])
    for store in stores:
        store.wait()


def hand_over(damped, spectrum, damped_out, spectrum_out, held_d, held_s, load_sem, store_sem):
    ways = []
    for x in range(0, NX, 2):
        for n in range(2):
            ways.append((damped, held_d, damped_out, n, x))
    for x in range(0, NX, 4):
        for n in range(2):
            ways.append((spectrum, held_s, spectrum_out, n, x))
    loads, stores = [], []
    for number, (source, held, target, n, x) in enumerate(ways):
        planes = pl.ds(x, 2 if source is damped else 4)
        loads.append(
            pltpu.make_async_copy(
                source.at[n, planes], held.at[n, planes], load_sem.at[number]
            )
        )
        stores.append(
            pltpu.make_async_copy(
                held.at[n, planes], target.at[n, planes], store_sem.at[number]
            )
        )
    for load in loads:
        load.start()
    for load, store in zip(loads, stores):
        load.wait()
        store.start()
    for store in stores:
        store.wait()


def phase_tables():
    n, k = np.arange(K)[:, None], np.arange(K)[None, :]
    angle = 2.0 * np.pi / K * ((n * k) % K) - np.pi * (n % 2)
    re, im = np.cos(angle), -np.sin(angle)
    along_y = np.block([[re.T, -im.T], [im.T, re.T]]).astype(np.float32)
    along_z = np.block([[re, im], [-im, re]]).astype(np.float32)
    found = []
    for table in (along_y, along_z):
        high = table.astype(BF)
        found += [high, (table - high.astype(np.float32)).astype(BF)]
    return np.stack(found)


def body(
    wavefunction,
    absorber,
    row_inverse,
    column_inverse,
    link_terms,
    shell_blocks,
    owner_map,
    volkov_phase,
):
    count = shell_blocks.shape[2]
    any_space = pl.BlockSpec(memory_space=pl.ANY)
    smem = pl.BlockSpec(memory_space=pltpu.SMEM)
    V = pltpu.VMEM
    dma = pltpu.SemaphoreType.DMA
    parts = len(PARTS)
    found = pl.pallas_call(
        kernel,
        out_shape=(
            jax.ShapeDtypeStruct((2, NX, CY, CZ), F32),
            jax.ShapeDtypeStruct((2, NX, K, K), F32),
        ),
        in_specs=[smem] + [pl.BlockSpec(memory_space=pltpu.HBM)] * 8,
        out_specs=(any_space, any_space),
        scratch_shapes=[
            V((2, NX, CY, CZ), F32),
            V((NX, CY, CZ), F32),
            V((2, CY, CY), F32),
            V((2, CZ, CZ), F32),
            V((2, NC, 8, CZ), F32),
            V((2, NC, 8, CZ), F32),
            V((NG, count), jnp.int32),
            V((NG, count), jnp.int32),
            V((K, K), F32),
            V((4, 2 * K, 2 * K), BF),
            V((2, 2 * CY, 2 * CY), BF),
            V((16, 2 * CY), F32),
            V((2, 16, 2 * CY), BF),
            V((4, CY, 128), F32),
            V((2, NX, 2 * CY, CZ), BF),
            V((UNITS, 4, 128), F32),
            V((NG, 4, 128), F32),
            V((1, 1, 128), F32),
            V((NG, 1, 128), F32),
            V((NG, 128), F32),
            V((4 * NG, 128), F32),
            V((4 * NG, 128), F32),
            V((NG, 4, 128), F32),
            V((UNITS, 4, 128), F32),
            V((NX, 2 * CY, CZ), F32),
            V((2, NX, CY, 2 * CZ), BF),
            V((2, 2 * CZ, 2 * CZ), BF),
            V((16, 2 * CZ), F32),
            V((2, 16, 2 * CZ), BF),
            V((PAIRS, 8, 128), F32),
            V((NC, PAIRS, 8, 128), F32),
            V((2, NC, 128), F32),
            V((4, NC, 128), F32),
            V((128, 128), F32),
            V((4, 2 * CZ), F32),
            V((2, 256, 2 * CZ), BF),
            V((2, NG, 128), F32),
            V((SLOT * NG, 2 * K), BF),
            V((2, NX, CY, CZ), F32),
            V((NX, NG, SLOT, 128), F32),
            V((NX, NG, SLOT, 128), F32),
            V((2, 2 * K, SLOT * NG), BF),
            V((2, K, K), F32),
            V((2, NX, K, K), F32),
            dma((9 + NX,)),
            dma((parts,)),
            dma((parts,)),
            dma((2,)),
            dma((2,)),
            dma((2,)),
            dma((parts,)),
            dma((parts,)),
            dma((parts,)),
            dma((parts,)),
        ],
        compiler_params=pltpu.CompilerParams(
            collective_id=0, has_side_effects=True, vmem_limit_bytes=60 * 1024 * 1024
        ),
    )(
        link_terms,
        wavefunction,
        absorber,
        row_inverse,
        column_inverse.reshape(2, NC, CZ, CZ),
        shell_blocks.reshape(NG, count),
        owner_map.reshape(NG, count),
        volkov_phase,
        phase_tables(),
    )
    return pl.pallas_call(
        hand_over,
        out_shape=tuple(jax.ShapeDtypeStruct(value.shape, F32) for value in found),
        in_specs=[any_space, any_space],
        out_specs=(any_space, any_space),
        scratch_shapes=[
            V((2, NX, CY, CZ), F32),
            V((2, NX, K, K), F32),
            dma((12,)),
            dma((12,)),
        ],
        compiler_params=pltpu.CompilerParams(vmem_limit_bytes=60 * 1024 * 1024),
    )(*found)


def solution(mesh):
    placed = (
        P(None, None, "gy", "gz"),
        P(None, "gy", "gz"),
        P(None, "gy", None),
        P(),
        P(),
        P("gz", None, None),
        P("gz", None, None, None),
        P(),
    )
    return jax.shard_map(
        body,
        mesh=mesh,
        in_specs=placed,
        out_specs=(P(None, None, "gy", "gz"), P(None, "gy", "gz", None)),
        check_vma=False,
    )
```

```python
import math

import jax
import jax.numpy as jnp
import numpy as np
from jax import lax
from jax.experimental import pallas as pl
from jax.experimental.pallas import tpu as pltpu
from jax.sharding import PartitionSpec as P

MESH = pl.DeviceIdType.MESH
BF = jnp.bfloat16
F32 = jnp.float32

NX = 8
PAIRS = 4
CY = 128
CZ = 256
K = 128
BY = 2
CAP = 4
SLOT = 2 * BY * CAP
NG = 32
NC = 8
UNITS = 16
PARTS = ((0, 1), (1, 3), (3, 4))


def split(value):
    high = value.astype(BF)
    return high, (value - high.astype(F32)).astype(BF)


NN = (((1,), (0,)), ((), ()))
NT = (((1,), (1,)), ((), ()))


def dot(a, b, dims=NN):
    return lax.dot_general(a, b, dims, preferred_element_type=F32)


def dot3(ah, al, bh, bl, dims=NN):
    return dot(ah, bh, dims) + dot(ah, bl, dims) + dot(al, bh, dims)


def cmul(a, b):
    return (a[0] * b[0] - a[1] * b[1], a[0] * b[1] + a[1] * b[0])


def cadd(a, b):
    return (a[0] + b[0], a[1] + b[1])


def cinv(a):
    modulus = a[0] * a[0] + a[1] * a[1]
    return (a[0] / modulus, -a[1] / modulus)


def chain(count, stride, edges):
    shape = (count, 128)
    place = lax.broadcasted_iota(jnp.int32, shape, 0)
    lane = lax.broadcasted_iota(jnp.int32, shape, 1) - stride * place
    one = jnp.ones(shape, F32)
    zero = jnp.zeros(shape, F32)
    head = ((lane == 0).astype(F32), (lane == 1).astype(F32))
    tail = ((lane == 2).astype(F32), (lane == 3).astype(F32))
    lead_left, tail_left, lead_right, tail_right = edges

    def shifted(value, by, fill):
        if by > 0:
            return jnp.where(place >= by, pltpu.roll(value, by, 0), fill)
        return jnp.where(place < count + by, pltpu.roll(value, count + by, 0), fill)

    def moved(value, by, fill):
        return (shifted(value[0], by, fill), shifted(value[1], by, zero))

    a, b = cmul(tail_left, lead_right), cmul(tail_right, lead_left)
    m = [(a[0] - b[0], a[1] - b[1]), tail_right, (-lead_left[0], -lead_left[1]), (one, zero)]
    by = 1
    while by < count:
        q = [moved(m[0], by, one), moved(m[1], by, zero), moved(m[2], by, zero), moved(m[3], by, one)]
        m = [
            cadd(cmul(m[0], q[0]), cmul(m[1], q[2])),
            cadd(cmul(m[0], q[1]), cmul(m[1], q[3])),
            cadd(cmul(m[2], q[0]), cmul(m[3], q[2])),
            cadd(cmul(m[2], q[1]), cmul(m[3], q[3])),
        ]
        by *= 2
    coupling = cmul(moved(m[1], 1, zero), cinv(moved(m[3], 1, one)))

    def affine(factor, addend, sign):
        by = 1
        while by < count:
            before = (moved(factor, sign * by, one), moved(addend, sign * by, zero))
            addend = cadd(cmul(factor, before[1]), addend)
            factor = cmul(factor, before[0])
            by *= 2
        return addend

    step = cmul(lead_left, coupling)
    inverse = cinv((1.0 - step[0], -step[1]))
    gain = cmul(tail_left, inverse)
    carried = moved(affine(gain, cadd(tail, cmul(cmul(gain, coupling), head)), 1), 1, zero)
    offset = cmul(cadd(head, cmul(lead_left, carried)), inverse)
    value = affine(cmul(lead_right, inverse), offset, -1)
    return cadd(carried, cmul(coupling, value)), moved(value, -1, zero)


def embed(target, size, real, imag):
    for n, piece in enumerate(split(real)):
        target[n, 0:size, 0:size] = piece
        target[n, size:, size:] = piece
    for n, piece in enumerate(split(imag)):
        target[n, 0:size, size:] = -piece
        target[n, size:, 0:size] = piece


def embed_edges(target, wide, size, source):
    wide[...] = jnp.zeros_like(wide)
    for n, r in enumerate((0, size - 1)):
        wide[2 * n : 2 * n + 1, 0:size] = source[0, r : r + 1, :]
        wide[2 * n : 2 * n + 1, size:] = -source[1, r : r + 1, :]
        wide[2 * n + 1 : 2 * n + 2, 0:size] = source[1, r : r + 1, :]
        wide[2 * n + 1 : 2 * n + 2, size:] = source[0, r : r + 1, :]
    target[0], target[1] = split(wide[...])


def rows_of(block):
    k = lax.broadcasted_iota(jnp.int32, (1, SLOT * NG), 1)
    row = (k // BY) % 2 * K + k % BY
    row = jnp.where(block > 0.5, row.astype(F32) + BY * (block - 1.0), -1.0)
    place = lax.broadcasted_iota(jnp.int32, (2 * K, SLOT * NG), 0).astype(F32)
    return (place == row).astype(F32)


def kernel(
    links,
    wave_hbm,
    absorber_hbm,
    row_hbm,
    column_hbm,
    blocks_hbm,
    owners_hbm,
    phase_hbm,
    tables_hbm,
    damped_hbm,
    spectrum_hbm,
    wave,
    absorber,
    row,
    column,
    top,
    bottom,
    listed,
    owners,
    phase,
    tables,
    yemb,
    ywide,
    yedge,
    spikes,
    psi,
    heads,
    gathered,
    edge_line,
    edges,
    edge_rows,
    flat_a,
    flat_v,
    values_out,
    values_in,
    solved,
    field,
    zemb,
    zwide,
    zedge,
    zheads,
    zall,
    zcorner,
    zresponse,
    square,
    zspike,
    zfix,
    padded,
    pick,
    damped,
    outgoing,
    incoming,
    ytab,
    volkov,
    spectrum,
    load_sem,
    damped_sem,
    spectrum_sem,
    edge_sem,
    head_sem,
    value_sem,
    z_send,
    z_recv,
    block_send,
    block_recv,
):
    me = lax.axis_index("gy")
    mez = lax.axis_index("gz")
    half = me // UNITS
    base = half * UNITS
    unit = me - base

    barrier = pltpu.get_barrier_semaphore()

    def greet(s, carry):
        pl.semaphore_signal(
            barrier, inc=1, device_id={"gy": lax.rem(me + s, NG)}, device_id_type=MESH
        )
        return carry

    def greet_z(s, carry):
        pl.semaphore_signal(
            barrier, inc=1, device_id={"gz": lax.rem(mez + s, NC)}, device_id_type=MESH
        )
        return carry

    def load(number, source, target):
        copy = pltpu.make_async_copy(source, target, load_sem.at[number])
        copy.start()
        return copy

    row_load = load(0, row_hbm, row)
    wave_loads = [load(9 + x, wave_hbm.at[:, x], wave.at[:, x]) for x in range(NX)]
    lax.fori_loop(1, NG, greet, 0)
    lax.fori_loop(1, NC, greet_z, 0)
    column_load = load(1, column_hbm.at[:, mez], column)
    top_load = load(2, column_hbm.at[:, :, pl.ds(0, 8), :], top)
    bottom_load = load(3, column_hbm.at[:, :, pl.ds(CZ - 8, 8), :], bottom)
    blocks_load = load(4, blocks_hbm, listed)
    owners_load = load(5, owners_hbm, owners)
    absorber_load = load(6, absorber_hbm, absorber)
    tables_load = load(7, tables_hbm, tables)
    phase_load = load(8, phase_hbm, phase)

    row_load.wait()
    embed_edges(yedge, ywide, CY, row)
    lane = lax.broadcasted_iota(jnp.int32, (1, 128), 1)
    edge_row = jnp.zeros((1, 128), F32)
    for side, place in enumerate((0, CY - 1)):
        link = (links[0, side, 0], links[0, side, 1])
        spike = cmul(link, (row[0, :, place : place + 1], row[1, :, place : place + 1]))
        for part in range(2):
            spikes[2 * side + part] = jnp.broadcast_to(spike[part], (CY, 128))
            for n, r in enumerate((0, CY - 1)):
                term = spikes[2 * side + part, r : r + 1, :]
                edge_row = jnp.where(lane == 4 * side + 2 * n + part, term, edge_row)
    edge_line[0] = edge_row

    for x in range(NX):
        wave_loads[x].wait()
        high, low = split(jnp.concatenate([wave[0, x], wave[1, x]], axis=0))
        psi[0, x], psi[1, x] = high, low
        found = dot3(yedge[0], yedge[1], high, low)
        for h in range(2):
            heads[2 * x + h] = found[0:4, 128 * h : 128 * h + 128]

    pl.semaphore_wait(barrier, NG - 1 + NC - 1)

    def send_edges(s, carry):
        pltpu.make_async_remote_copy(
            src_ref=edge_line,
            dst_ref=edges.at[pl.ds(me, 1)],
            send_sem=edge_sem.at[0],
            recv_sem=edge_sem.at[1],
            device_id={"gy": lax.rem(me + s, NG)},
            device_id_type=MESH,
        ).start()
        return carry

    lax.fori_loop(1, NG, send_edges, 0, unroll=True)
    edges[me] = edge_row

    def send_heads(s, carry):
        peer = lax.rem(me + s, NG)
        pltpu.make_async_remote_copy(
            src_ref=heads.at[lax.rem(peer, UNITS)],
            dst_ref=gathered.at[me],
            send_sem=head_sem.at[0],
            recv_sem=head_sem.at[1],
            device_id={"gy": peer},
            device_id_type=MESH,
        ).start()
        return carry

    lax.fori_loop(1, NG, send_heads, 0, unroll=True)
    gathered[me] = heads[unit]

    pltpu.make_async_copy(
        edges.at[pl.ds(0, NG - 1)], edges.at[pl.ds(0, NG - 1)], edge_sem.at[1]
    ).wait()
    for j in range(NG):
        edge_rows[j : j + 1, :] = edges[j]
    wide = [jnp.broadcast_to(edge_rows[:, i : i + 1], (NG, 128)) for i in range(8)]
    left, right = chain(NG, 4, [(wide[i], wide[i + 1]) for i in (0, 2, 4, 6)])
    for i, value in enumerate(left + right):
        flat_a[pl.ds(i, NG, stride=4), :] = value
    embed(yemb, CY, row[0], row[1])
    for x in range(NX):
        solved[x] = dot3(yemb[0], yemb[1], psi[0, x], psi[1, x])

    pltpu.make_async_copy(
        gathered.at[pl.ds(0, NG - 1)], gathered.at[pl.ds(0, NG - 1)], head_sem.at[1]
    ).wait()
    for j in range(NG):
        flat_v[4 * j : 4 * j + 4, :] = gathered[j]
    ah, al = split(flat_a[...])
    vh, vl = split(flat_v[...])
    found = dot3(ah, al, vh, vl)
    for j in range(NG):
        values_out[j] = found[4 * j : 4 * j + 4, :]

    def send_values(s, carry):
        peer = base + lax.rem(unit + s, UNITS)
        pltpu.make_async_remote_copy(
            src_ref=values_out.at[peer],
            dst_ref=values_in.at[unit],
            send_sem=value_sem.at[0],
            recv_sem=value_sem.at[1],
            device_id={"gy": peer},
            device_id_type=MESH,
        ).start()
        return carry

    lax.fori_loop(1, UNITS, send_values, 0, unroll=True)
    values_in[unit] = values_out[me]

    column_load.wait()
    embed(zemb, CZ, column[0], column[1])
    embed_edges(zedge, zwide, CZ, column)
    for side in range(2):
        link = (links[1, side, 0], links[1, side, 1])
        lines = []
        for part in range(2):
            pieces = []
            for a in range(2):
                turned = jnp.transpose(
                    column[part, 128 * a : 128 * a + 128, 128 * side : 128 * side + 128]
                )
                pieces.append(turned[0:1, :] if side == 0 else turned[127:128, :])
            lines.append(jnp.concatenate(pieces, axis=1))
        spike = cmul(link, (lines[0], lines[1]))
        zspike[2 * side : 2 * side + 1, 0:CZ] = spike[0]
        zspike[2 * side : 2 * side + 1, CZ:] = spike[1]
        zspike[2 * side + 1 : 2 * side + 2, 0:CZ] = -spike[1]
        zspike[2 * side + 1 : 2 * side + 2, CZ:] = spike[0]

    top_load.wait()
    bottom_load.wait()
    terms = []
    for side, place in enumerate((0, CZ - 1)):
        link = (links[1, side, 0], links[1, side, 1])
        for table, r in ((top, 0), (bottom, 7)):
            for part in range(2):
                for c in range(NC):
                    lanes = 128 * side
                    zcorner[part, c : c + 1, :] = table[part, c, r : r + 1, lanes : lanes + 128]
            at = place % 128
            value = tuple(
                jnp.broadcast_to(zcorner[part][:, at : at + 1], (NC, 128)) for part in range(2)
            )
            terms.append(cmul(link, value))
    left, right = chain(NC, 8, terms)
    square[...] = jnp.zeros_like(square)
    for i, value in enumerate(left + right):
        zresponse[i] = value
        square[i : i + 1, :] = zresponse[i, pl.ds(mez, 1), :]
    turned = jnp.transpose(square[...])
    held = jnp.zeros((64, 2 * CZ), F32)
    for i in range(4):
        held = held + turned[0:64, i : i + 1] * zspike[i : i + 1, :]
    for h in range(2):
        high, low = split(held if h == 0 else pltpu.roll(held, 4, 0))
        zfix[h, 0:64, :] = high
        zfix[h, 64:128, :] = high
        zfix[h, 128:192, :] = low
        zfix[h, 192:256, :] = low

    blocks_load.wait()
    owners_load.wait()
    padded[...] = jnp.full_like(padded, -1.0)
    count = listed.shape[1]
    padded[0, :, 0:count] = listed[...].astype(F32)
    padded[1, :, 0:count] = owners[...].astype(F32)
    ids, names = (
        jnp.transpose(jnp.broadcast_to(padded[n, pl.ds(me, 1), :], (128, 128))) for n in range(2)
    )
    across = lax.broadcasted_iota(jnp.int32, (128, 128), 1)
    down = lax.broadcasted_iota(jnp.int32, (128, 128), 0)
    same = (names == padded[1, pl.ds(me, 1), :]) & (across < down)
    rank = jnp.sum(same.astype(F32), axis=1, keepdims=True)
    slot = jnp.where(names[:, 0:1] < 0.0, -1.0, CAP * names[:, 0:1] + rank)
    k = lax.broadcasted_iota(jnp.int32, (1, SLOT * NG), 1)
    hit = slot == (k // (2 * BY)).astype(F32)
    block = jnp.sum(jnp.where(hit, ids[:, 0:1] + 1.0, 0.0), axis=0, keepdims=True)
    onehot = rows_of(block)
    for n in range(SLOT * NG // 128):
        for m in range(2):
            pick[128 * n : 128 * n + 128, 128 * m : 128 * m + 128] = jnp.transpose(
                onehot[128 * m : 128 * m + 128, 128 * n : 128 * n + 128]
            ).astype(BF)

    pltpu.make_async_copy(
        values_in.at[pl.ds(0, UNITS - 1)], values_in.at[pl.ds(0, UNITS - 1)], value_sem.at[1]
    ).wait()

    def meet_z(part):
        first, last = PARTS[part]
        for p in range(first, last):
            for x in (2 * p, 2 * p + 1):
                for h in range(2):
                    v = values_in[2 * x + h]
                    lre, lim, rre, rim = (v[i : i + 1, :] for i in range(4))
                    re = solved[x, 0:CY, 128 * h : 128 * h + 128]
                    im = solved[x, CY:, 128 * h : 128 * h + 128]
                    re = re + (spikes[0] * lre - spikes[1] * lim)
                    re = re + (spikes[2] * rre - spikes[3] * rim)
                    im = im + (spikes[0] * lim + spikes[1] * lre)
                    im = im + (spikes[2] * rim + spikes[3] * rre)
                    for c, value in enumerate((re, im)):
                        high, low = split(value)
                        at = CZ * c + 128 * h
                        field[0, x, :, at : at + 128] = high
                        field[1, x, :, at : at + 128] = low
                found = dot3(zedge[0], zedge[1], field[0, x], field[1, x], NT)
                zheads[p, 4 * (x % 2) : 4 * (x % 2) + 4, :] = found[0:4, :]

        def send_zheads(s, carry):
            pltpu.make_async_remote_copy(
                src_ref=zheads.at[pl.ds(first, last - first)],
                dst_ref=zall.at[mez, pl.ds(first, last - first)],
                send_sem=z_send.at[part],
                recv_sem=z_recv.at[part],
                device_id={"gz": lax.rem(mez + s, NC)},
                device_id_type=MESH,
            ).start()
            return carry

        lax.fori_loop(1, NC, send_zheads, 0, unroll=True)
        for p in range(first, last):
            zall[mez, p] = zheads[p]

    stores = []
    meet_z(0)
    for part, (first, last) in enumerate(PARTS):
        if part + 1 < len(PARTS):
            meet_z(part + 1)
        planes = pl.ds(2 * first, 2 * (last - first))
        for x in range(2 * first, 2 * last):
            solved[x, 0:CY, :] = dot3(
                field[0, x], field[1, x], zemb[0, 0:CZ, :], zemb[1, 0:CZ, :], NT
            )
            solved[x, CY:, :] = dot3(
                field[0, x], field[1, x], zemb[0, CZ:, :], zemb[1, CZ:, :], NT
            )
        if part == 0:
            absorber_load.wait()
        view = zall.at[pl.ds(0, NC - 1), pl.ds(first, last - first)]
        pltpu.make_async_copy(view, view, z_recv.at[part]).wait()
        for p in range(first, last):
            g = zall[:, p].reshape(8 * NC, 128)
            high = g.astype(BF).astype(F32)
            turned = jnp.transpose(jnp.concatenate([high, g - high], axis=0)).astype(BF)
            turned = jnp.concatenate([turned, turned], axis=1)
            folded = []
            for x in (2 * p, 2 * p + 1):
                fix = dot(turned, zfix[x % 2])
                kept = jnp.exp(-absorber[x])
                rows = []
                for c in range(2):
                    value = solved[x, CY * c : CY * c + CY, :] + fix[:, CZ * c : CZ * c + CZ]
                    left = value * kept
                    damped[c, x] = left
                    lost = value - left
                    rows.append(lost[:, 0:128] + lost[:, 128:256])
                folded.append(jnp.concatenate(rows, axis=0))
            high, low = split(jnp.concatenate(folded, axis=1))
            chosen = dot(pick[...], high) + dot(pick[...], low)
            for n in range(2):
                outgoing[2 * p + n] = chosen[:, 128 * n : 128 * n + 128].reshape(NG, SLOT, 128)

        def send_blocks(s, carry):
            peer = lax.rem(me + s, NG)
            pltpu.make_async_remote_copy(
                src_ref=outgoing.at[planes, peer],
                dst_ref=incoming.at[planes, me],
                send_sem=block_send.at[part],
                recv_sem=block_recv.at[part],
                device_id={"gy": peer},
                device_id_type=MESH,
            ).start()
            return carry

        lax.fori_loop(1, NG, send_blocks, 0)
        for x in range(2 * first, 2 * last):
            incoming[x, me] = outgoing[x, me]
        store = pltpu.make_async_copy(
            damped.at[:, planes], damped_hbm.at[:, planes], damped_sem.at[part]
        )
        store.start()
        stores.append(store)

    source = lax.broadcasted_iota(jnp.int32, (NG, SLOT * NG), 0)
    mine = (padded[1] == me.astype(F32)).astype(F32)
    rank = dot(mine.astype(BF), (down < across).astype(F32).astype(BF))
    total = jnp.zeros((NG, SLOT * NG), F32)
    for n in range(CAP):
        hit = jnp.where(rank == float(n), mine, 0.0)
        found = jnp.sum(hit * (padded[0] + 1.0), axis=1, keepdims=True)
        total = total + jnp.where((k // (2 * BY)) % CAP == n, found, 0.0)
    total = jnp.where(k // SLOT == source, total, 0.0)
    onehot = rows_of(jnp.sum(total, axis=0, keepdims=True)).astype(BF)
    tables_load.wait()
    for n in range(2):
        ytab[n] = dot(tables[n], onehot).astype(BF)
    phase_load.wait()
    norm = 1.0 / math.sqrt(CY * CZ)
    volkov[0] = jnp.cos(phase[...])
    volkov[1] = jnp.sin(phase[...])

    for part, (first, last) in enumerate(PARTS):
        planes = pl.ds(2 * first, 2 * (last - first))
        view = incoming.at[planes, pl.ds(0, NG - 1)]
        pltpu.make_async_copy(view, view, block_recv.at[part]).wait()
        for p in range(first, last):
            both = [incoming[2 * p + n].reshape(SLOT * NG, 128) for n in range(2)]
            high, low = split(jnp.concatenate(both, axis=1))
            along_y = dot3(ytab[0], ytab[1], high, low)
            lines = [
                jnp.concatenate(
                    [along_y[0:K, 128 * n : 128 * n + 128], along_y[K:, 128 * n : 128 * n + 128]],
                    axis=1,
                )
                for n in range(2)
            ]
            high, low = split(jnp.concatenate(lines, axis=0))
            both = dot3(high, low, tables[2], tables[3])
            for n in range(2):
                value = (both[K * n : K * n + K, 0:K], both[K * n : K * n + K, K:])
                re, im = cmul((volkov[0], volkov[1]), value)
                spectrum[0, 2 * p + n] = re * norm
                spectrum[1, 2 * p + n] = im * norm
        store = pltpu.make_async_copy(
            spectrum.at[:, planes], spectrum_hbm.at[:, planes], spectrum_sem.at[part]
        )
        store.start()
        stores.append(store)

    def sent(view, sem):
        pltpu.make_async_copy(view, view, sem).wait()

    sent(edges.at[pl.ds(0, NG - 1)], edge_sem.at[0])
    sent(gathered.at[pl.ds(0, NG - 1)], head_sem.at[0])
    sent(values_in.at[pl.ds(0, UNITS - 1)], value_sem.at[0])
    for part, (first, last) in enumerate(PARTS):
        sent(zall.at[pl.ds(0, NC - 1), pl.ds(first, last - first)], z_send.at[part])
        planes = pl.ds(2 * first, 2 * (last - first))
        sent(outgoing.at[planes, pl.ds(0, NG - 1)], block_send.at[part])
    for store in stores:
        store.wait()


def hand_over(damped, spectrum, damped_out, spectrum_out, held_d, held_s, load_sem, store_sem):
    ways = []
    for x in range(0, NX, 2):
        for n in range(2):
            ways.append((damped, held_d, damped_out, n, x))
    for x in range(0, NX, 4):
        for n in range(2):
            ways.append((spectrum, held_s, spectrum_out, n, x))
    loads, stores = [], []
    for number, (source, held, target, n, x) in enumerate(ways):
        planes = pl.ds(x, 2 if source is damped else 4)
        loads.append(
            pltpu.make_async_copy(
                source.at[n, planes], held.at[n, planes], load_sem.at[number]
            )
        )
        stores.append(
            pltpu.make_async_copy(
                held.at[n, planes], target.at[n, planes], store_sem.at[number]
            )
        )
    for load in loads:
        load.start()
    for load, store in zip(loads, stores):
        load.wait()
        store.start()
    for store in stores:
        store.wait()


def phase_tables():
    n, k = np.arange(K)[:, None], np.arange(K)[None, :]
    angle = 2.0 * np.pi / K * ((n * k) % K) - np.pi * (n % 2)
    re, im = np.cos(angle), -np.sin(angle)
    along_y = np.block([[re.T, -im.T], [im.T, re.T]]).astype(np.float32)
    along_z = np.block([[re, im], [-im, re]]).astype(np.float32)
    found = []
    for table in (along_y, along_z):
        high = table.astype(BF)
        found += [high, (table - high.astype(np.float32)).astype(BF)]
    return np.stack(found)


def body(
    wavefunction,
    absorber,
    row_inverse,
    column_inverse,
    link_terms,
    shell_blocks,
    owner_map,
    volkov_phase,
):
    count = shell_blocks.shape[2]
    any_space = pl.BlockSpec(memory_space=pl.ANY)
    smem = pl.BlockSpec(memory_space=pltpu.SMEM)
    V = pltpu.VMEM
    dma = pltpu.SemaphoreType.DMA
    parts = len(PARTS)
    found = pl.pallas_call(
        kernel,
        out_shape=(
            jax.ShapeDtypeStruct((2, NX, CY, CZ), F32),
            jax.ShapeDtypeStruct((2, NX, K, K), F32),
        ),
        in_specs=[smem] + [pl.BlockSpec(memory_space=pltpu.HBM)] * 8,
        out_specs=(any_space, any_space),
        scratch_shapes=[
            V((2, NX, CY, CZ), F32),
            V((NX, CY, CZ), F32),
            V((2, CY, CY), F32),
            V((2, CZ, CZ), F32),
            V((2, NC, 8, CZ), F32),
            V((2, NC, 8, CZ), F32),
            V((NG, count), jnp.int32),
            V((NG, count), jnp.int32),
            V((K, K), F32),
            V((4, 2 * K, 2 * K), BF),
            V((2, 2 * CY, 2 * CY), BF),
            V((16, 2 * CY), F32),
            V((2, 16, 2 * CY), BF),
            V((4, CY, 128), F32),
            V((2, NX, 2 * CY, CZ), BF),
            V((UNITS, 4, 128), F32),
            V((NG, 4, 128), F32),
            V((1, 1, 128), F32),
            V((NG, 1, 128), F32),
            V((NG, 128), F32),
            V((4 * NG, 128), F32),
            V((4 * NG, 128), F32),
            V((NG, 4, 128), F32),
            V((UNITS, 4, 128), F32),
            V((NX, 2 * CY, CZ), F32),
            V((2, NX, CY, 2 * CZ), BF),
            V((2, 2 * CZ, 2 * CZ), BF),
            V((16, 2 * CZ), F32),
            V((2, 16, 2 * CZ), BF),
            V((PAIRS, 8, 128), F32),
            V((NC, PAIRS, 8, 128), F32),
            V((2, NC, 128), F32),
            V((4, NC, 128), F32),
            V((128, 128), F32),
            V((4, 2 * CZ), F32),
            V((2, 256, 2 * CZ), BF),
            V((2, NG, 128), F32),
            V((SLOT * NG, 2 * K), BF),
            V((2, NX, CY, CZ), F32),
            V((NX, NG, SLOT, 128), F32),
            V((NX, NG, SLOT, 128), F32),
            V((2, 2 * K, SLOT * NG), BF),
            V((2, K, K), F32),
            V((2, NX, K, K), F32),
            dma((9 + NX,)),
            dma((parts,)),
            dma((parts,)),
            dma((2,)),
            dma((2,)),
            dma((2,)),
            dma((parts,)),
            dma((parts,)),
            dma((parts,)),
            dma((parts,)),
        ],
        compiler_params=pltpu.CompilerParams(
            collective_id=0, has_side_effects=True, vmem_limit_bytes=60 * 1024 * 1024
        ),
    )(
        link_terms,
        wavefunction,
        absorber,
        row_inverse,
        column_inverse.reshape(2, NC, CZ, CZ),
        shell_blocks.reshape(NG, count),
        owner_map.reshape(NG, count),
        volkov_phase,
        phase_tables(),
    )
    return pl.pallas_call(
        hand_over,
        out_shape=tuple(jax.ShapeDtypeStruct(value.shape, F32) for value in found),
        in_specs=[any_space, any_space],
        out_specs=(any_space, any_space),
        scratch_shapes=[
            V((2, NX, CY, CZ), F32),
            V((2, NX, K, K), F32),
            dma((12,)),
            dma((12,)),
        ],
        compiler_params=pltpu.CompilerParams(vmem_limit_bytes=60 * 1024 * 1024),
    )(*found)


def solution(mesh):
    placed = (
        P(None, None, "gy", "gz"),
        P(None, "gy", "gz"),
        P(None, "gy", None),
        P(),
        P(),
        P("gz", None, None),
        P("gz", None, None, None),
        P(),
    )
    return jax.shard_map(
        body,
        mesh=mesh,
        in_specs=placed,
        out_specs=(P(None, None, "gy", "gz"), P(None, "gy", "gz", None)),
        check_vma=False,
    )
```
